32 devices in a mesh: ctx: 16 (over z, y, x), head: 2 (over core).
Axes of the slice: x: 2, y: 2, z: 4, core: 2. Of those that a mesh axis runs over, the one named last changes fastest.
Arguments:
- content_rows: bfloat16 [4, 128, 4, 2048], P(None, 'ctx'), may hold values from -6 to 6
- w_hidden: bfloat16 [2048, 4096], P(None, 'head'), may hold values from -0.125 to 0.125
- w_embed: bfloat16 [4096, 512], P('head'), may hold values from -0.09375 to 0.09375
- w_query: bfloat16 [512, 512], P(None, 'head'), may hold values from -0.25 to 0.25
- w_gate: bfloat16 [512, 512], P(None, 'head'), may hold values from -0.25 to 0.25
- w_proj: bfloat16 [512, 512], P('head'), may hold values from -0.25 to 0.25
- history_keys: bfloat16 [4, 36864, 512], P(None, 'ctx', 'head'), may hold values from -6 to 6
- history_values: bfloat16 [4, 36864, 512], P(None, 'ctx', 'head'), may hold values from -6 to 6
- cutoffs: int32 [4, 128], replicated, may hold values from 9216 to 36864
- out_cotangent: bfloat16 [4, 128, 512], P(None, 'ctx'), may hold values from -6 to 6
Outputs:
- content_grad: bfloat16 [4, 128, 4, 2048], P(None, 'ctx', 'head')
The draws below stay inside these ranges and needn't reach their ends.
Inputs may be any that keep to these rules, and one draw needn't show every extreme that they name: cutoffs[u, t] counts the leading events of user u's history that its target t sees.
All inputs are finite; a program needn't handle non-finite values.
Results may differ from the reference program's by a relative error of at most 0.02.
Values may be sent and summed in bfloat16 or wider, within the bound.
No kernel may reach another device: no remote copies, remote signals or barrier semaphores. Data moves between devices by JAX's collectives and lax.ppermute only.
A program may use at most 128 MiB of HBM per device.

```python
import jax
import jax.numpy as jnp
from jax import lax

D = 512
HEADS = 4
DH = 128
CONTENT = 2048
MLP_HID = 4096
CONTENT_ROWS = 4
USERS = 4
EV_DEV = 2304
TGT_USER = 128
HIST_LEN = 36864


def place_ends(values, key, low, high):
    longest = values.shape.index(max(values.shape))
    spots = []
    for shift in (0, 1):
        where = [jax.random.randint(jax.random.fold_in(key, axis), (), 0, length) for axis, length in enumerate(values.shape)]
        where[longest] = (where[longest] + shift) % values.shape[longest]
        spots.append(tuple(where))
    return values.at[spots[0]].set(low).at[spots[1]].set(high)


def block_levels(rng, shape, split, least, largest):
    def one(dim, parts):
        steps = jax.random.uniform(jax.random.fold_in(jax.random.fold_in(rng, 6), dim), (parts,), jnp.float32, least / len(split), largest / len(split))
        return jnp.repeat(jnp.exp(steps), shape[dim] // parts).reshape((-1,) + (1,) * (len(shape) - dim - 1))

    level = one(*split[0])
    for cut in split[1:]:
        level = level * one(*cut)
    return level


def scatter_about(rng, shape, spread, reach, pieces=(), kind=jnp.bfloat16):
    drawn = spread * jax.random.normal(rng, shape, jnp.float32)
    if pieces:
        drawn = drawn * block_levels(rng, shape, pieces, -0.22, 0.18)
    return jnp.clip(drawn, -reach, reach).astype(kind)


def setup_inputs(seed: int = 0) -> dict:
    keys = jax.random.split(jax.random.key(seed), 11)
    content_rows = scatter_about(keys[0], (USERS, TGT_USER, CONTENT_ROWS, CONTENT), 1.0, 6.0, ((1, 16),))
    w_hidden = scatter_about(keys[1], (CONTENT, MLP_HID), CONTENT ** -0.5, 0.125, ((1, 2),))
    w_embed = scatter_about(keys[2], (MLP_HID, D), MLP_HID ** -0.5, 0.09375, ((0, 2),))
    w_query = scatter_about(keys[3], (D, D), D ** -0.5, 0.25, ((1, 2),))
    w_gate = scatter_about(keys[4], (D, D), D ** -0.5, 0.25, ((1, 2),))
    w_proj = scatter_about(keys[5], (D, D), D ** -0.5, 0.25, ((0, 2),))
    history_keys = scatter_about(keys[6], (USERS, HIST_LEN, D), 1.0, 6.0, ((1, 16), (2, 2)))
    history_values = scatter_about(keys[7], (USERS, HIST_LEN, D), 1.0, 6.0, ((1, 16), (2, 2)))
    cutoffs = place_ends(jax.random.randint(keys[8], (USERS, TGT_USER), HIST_LEN // 4, HIST_LEN + 1), jax.random.fold_in(keys[8], 1), HIST_LEN // 4, HIST_LEN).astype(jnp.int32)
    out_cotangent = scatter_about(keys[9], (USERS, TGT_USER, D), 1.0, 6.0, ((1, 16),))
    return {"content_rows": content_rows, "w_hidden": w_hidden, "w_embed": w_embed, "w_query": w_query, "w_gate": w_gate, "w_proj": w_proj, "history_keys": history_keys, "history_values": history_values, "cutoffs": cutoffs, "out_cotangent": out_cotangent}


def silu_slope(values_in):
    sigmoid_part = jax.nn.sigmoid(values_in)
    return sigmoid_part * (1.0 + values_in * (1.0 - sigmoid_part))

def contract_last(left, right):
    return lax.dot_general(left, right, (((1,), (1,)), ((), ())), preferred_element_type=jnp.float32)

def reference(content_rows, w_hidden, w_embed, w_query, w_gate, w_proj, history_keys, history_values, cutoffs, out_cotangent):
    flat_rows = content_rows.reshape(-1, CONTENT)
    hidden_lin = jnp.dot(flat_rows, w_hidden, preferred_element_type=jnp.float32)
    hidden = jax.nn.silu(hidden_lin).astype(jnp.bfloat16)
    encoded = jnp.dot(hidden, w_embed, preferred_element_type=jnp.float32)
    encoded = encoded.reshape(USERS * TGT_USER, CONTENT_ROWS, D)
    embedded = (0.5 * lax.optimization_barrier(jnp.sum(encoded, axis=1))).astype(jnp.bfloat16)
    query_lin = jnp.dot(embedded, w_query, preferred_element_type=jnp.float32)
    gate_lin = jnp.dot(embedded, w_gate, preferred_element_type=jnp.float32)
    queries = jax.nn.silu(query_lin).astype(jnp.bfloat16).reshape(USERS, TGT_USER, HEADS, DH)
    gates = jax.nn.silu(gate_lin).astype(jnp.bfloat16)
    out_grad = contract_last(out_cotangent.reshape(-1, D), w_proj).astype(jnp.bfloat16)
    score_scale = DH ** (-0.5)
    blocks = HIST_LEN // EV_DEV
    starts = jnp.arange(blocks, dtype=jnp.int32) * EV_DEV
    key_heads = history_keys.reshape(USERS, blocks, EV_DEV, HEADS, DH)
    value_heads = history_values.reshape(USERS, blocks, EV_DEV, HEADS, DH)

    def forward_user(packed):
        user_queries, limits, user_keys, user_values = packed
        query_float = user_queries.astype(jnp.float32)

        def block_step(total, inputs):
            block_keys, block_values, start = inputs
            scores = jnp.einsum('thd,phd->htp', query_float, block_keys.astype(jnp.float32)) * score_scale
            positions = start + jnp.arange(EV_DEV, dtype=jnp.int32)
            visible = positions[None, :] < limits[:, None]
            weights = jnp.where(visible[None], jax.nn.silu(scores), 0.0).astype(jnp.bfloat16)
            return (total + jnp.einsum('htp,phd->thd', weights.astype(jnp.float32), block_values.astype(jnp.float32)), None)
        begin = jnp.zeros((TGT_USER, HEADS, DH), jnp.float32)
        total, unused = lax.scan(block_step, begin, (user_keys, user_values, starts))
        return total
    attended = lax.map(forward_user, (queries, cutoffs, key_heads, value_heads))
    rscale = lax.rsqrt(lax.optimization_barrier(jnp.mean(attended * attended, axis=-1, keepdims=True)) + 1e-06)
    normed = attended * rscale
    grad_heads = out_grad.reshape(USERS, TGT_USER, HEADS, DH).astype(jnp.float32)
    gate_heads = gates.reshape(USERS, TGT_USER, HEADS, DH).astype(jnp.float32)
    gate_grad = grad_heads * normed
    normed_grad = grad_heads * gate_heads
    attn_grad = (rscale * (normed_grad - normed * lax.optimization_barrier(jnp.mean(normed_grad * normed, axis=-1, keepdims=True)))).astype(jnp.bfloat16)

    def backward_user(packed):
        user_queries, limits, user_keys, user_values, user_grads = packed
        query_float = user_queries.astype(jnp.float32)
        grad_float = user_grads.astype(jnp.float32)

        def block_step(total, inputs):
            block_keys, block_values, start = inputs
            keys_float = block_keys.astype(jnp.float32)
            scores = jnp.einsum('thd,phd->htp', query_float, keys_float) * score_scale
            positions = start + jnp.arange(EV_DEV, dtype=jnp.int32)
            visible = positions[None, :] < limits[:, None]
            weight_grad = jnp.einsum('thd,phd->htp', grad_float, block_values.astype(jnp.float32))
            grad_scores = jnp.where(visible[None], weight_grad * silu_slope(scores), 0.0).astype(jnp.bfloat16)
            return (total + jnp.einsum('htp,phd->thd', grad_scores.astype(jnp.float32), keys_float), None)
        begin = jnp.zeros((TGT_USER, HEADS, DH), jnp.float32)
        total, unused = lax.scan(block_step, begin, (user_keys, user_values, starts))
        return total * score_scale
    query_grad = lax.map(backward_user, (queries, cutoffs, key_heads, value_heads, attn_grad))
    query_back = (query_grad.reshape(-1, D) * silu_slope(query_lin)).astype(jnp.bfloat16)
    gate_back = (gate_grad.reshape(-1, D) * silu_slope(gate_lin)).astype(jnp.bfloat16)
    embed_total = contract_last(query_back, w_query) + contract_last(gate_back, w_gate)
    embed_grad = (0.5 * embed_total).astype(jnp.bfloat16)
    hidden_grad = contract_last(embed_grad, w_embed)
    slopes = silu_slope(hidden_lin).reshape(USERS * TGT_USER, CONTENT_ROWS, MLP_HID)
    hidden_back = (hidden_grad[:, None, :] * slopes).astype(jnp.bfloat16).reshape(-1, MLP_HID)
    content_grad = contract_last(hidden_back, w_hidden).astype(jnp.bfloat16)
    return content_grad.reshape(USERS, TGT_USER, CONTENT_ROWS, CONTENT)
```

```python
import functools

import jax
import jax.numpy as jnp
from jax import lax
from jax.experimental import pallas as pl
from jax.experimental.pallas import tpu as pltpu
from jax.sharding import PartitionSpec as P

DH = 128
F32 = jnp.float32
BF16 = jnp.bfloat16


def matmul(left, right):
    return jnp.dot(left, right, preferred_element_type=F32)


def contract_last(left, right):
    return lax.dot_general(left, right, (((1,), (1,)), ((), ())), preferred_element_type=F32)


def silu_parts(half):
    tanh = jnp.tanh(half)
    value = half + half * tanh
    slope = 0.5 * (1.0 + tanh) * (1.0 + half * (1.0 - tanh))
    return value, slope


def whole(shape):
    return pl.BlockSpec(shape, lambda *_: (0,) * len(shape))


def params(*semantics):
    return pltpu.CompilerParams(dimension_semantics=semantics, vmem_limit_bytes=40 << 20)


def encode_kernel(parts, rows_ref, wh_ref, we_ref, slope_ref, out_ref, acc_ref):
    step = pl.program_id(0)
    lin = matmul(rows_ref[...], wh_ref[...])
    value, slope = silu_parts(0.5 * lin)
    slope_ref[...] = slope
    part = matmul(value.astype(BF16), we_ref[...])

    @pl.when(step == 0)
    def _():
        acc_ref[...] = part

    @pl.when(step > 0)
    def _():
        acc_ref[...] += part

    @pl.when(step == pl.num_programs(0) - 1)
    def _():
        count = out_ref.shape[0]
        total = acc_ref[0:count]
        for part_index in range(1, parts):
            total = total + acc_ref[part_index * count : (part_index + 1) * count]
        out_ref[...] = total


def encode(rows, w_hidden, w_embed, parts, block):
    count, width = rows.shape
    hidden = w_hidden.shape[1]
    model = w_embed.shape[1]
    return pl.pallas_call(
        functools.partial(encode_kernel, parts),
        grid=(hidden // block,),
        in_specs=[
            whole(rows.shape),
            pl.BlockSpec((width, block), lambda j: (0, j)),
            pl.BlockSpec((block, model), lambda j: (j, 0)),
        ],
        out_specs=[
            pl.BlockSpec((count, block), lambda j: (0, j)),
            whole((count // parts, model)),
        ],
        out_shape=[
            jax.ShapeDtypeStruct((count, hidden), F32),
            jax.ShapeDtypeStruct((count // parts, model), F32),
        ],
        scratch_shapes=[pltpu.VMEM((count, model), F32)],
        compiler_params=params("arbitrary"),
        name="encode",
    )(rows, w_hidden, w_embed)


def project_kernel(
    mine_ref, other_ref, wq_ref, wg_ref, wp_ref, cot_ref, send_ref, gates_ref, og_ref, qs_ref, gs_ref
):
    embedded = (0.5 * (mine_ref[...] + other_ref[...])).astype(BF16)
    query, query_slope = silu_parts(0.5 * matmul(embedded, wq_ref[...]))
    gate, gate_slope = silu_parts(0.5 * matmul(embedded, wg_ref[...]))
    qs_ref[...] = query_slope
    gs_ref[...] = gate_slope
    gates_ref[...] = gate.astype(BF16).astype(F32)
    og_ref[...] = contract_last(cot_ref[...], wp_ref[...]).astype(BF16).astype(F32)
    block = query.reshape(send_ref.shape[1:]).astype(BF16)
    for index in range(send_ref.shape[0]):
        send_ref[index] = block


def project(mine, other, w_query, w_gate, w_proj, cotangent, copies, users):
    count = mine.shape[0]
    local = w_query.shape[1]
    rows = jax.ShapeDtypeStruct((count, local), F32)
    return pl.pallas_call(
        project_kernel,
        out_shape=[jax.ShapeDtypeStruct((copies, users, count // users, local), BF16)] + [rows] * 4,
        compiler_params=params(),
        name="project",
    )(mine, other, w_query, w_gate, w_proj, cotangent)


def forward_kernel(scale, heads, query_ref, limit_ref, key_ref, value_ref, out_ref, slope_ref, q_ref, acc_ref):
    step = pl.program_id(1)

    @pl.when(step == 0)
    def _():
        q_ref[...] = query_ref[...].astype(F32).reshape(q_ref.shape).astype(BF16)
        acc_ref[...] = jnp.zeros_like(acc_ref)

    targets, events = q_ref.shape[0], key_ref.shape[1]
    spots = lax.broadcasted_iota(jnp.int32, (targets, events), 1) + step * events
    visible = spots < limit_ref[0]
    for head in range(heads):
        lanes = slice(head * DH, (head + 1) * DH)
        half = contract_last(q_ref[:, lanes], key_ref[0, :, lanes]) * (0.5 * scale)
        value, slope = silu_parts(half)
        weights = jnp.where(visible, value, 0.0).astype(BF16)
        slope_ref[0, head] = jnp.where(visible, slope, 0.0).astype(BF16)
        acc_ref[:, lanes] += matmul(weights, value_ref[0, :, lanes])

    @pl.when(step == pl.num_programs(1) - 1)
    def _():
        out_ref[...] = acc_ref[...].reshape(out_ref.shape).astype(BF16)


def forward_attention(queries, limits, keys, values, heads, block):
    copies, users, rows, local = queries.shape
    events = keys.shape[1]
    targets = copies * rows
    spread = pl.BlockSpec((copies, 1, rows, local), lambda u, e: (0, u, 0, 0))
    event_block = pl.BlockSpec((1, block, local), lambda u, e: (u, e, 0))
    return pl.pallas_call(
        functools.partial(forward_kernel, DH ** (-0.5), heads),
        grid=(users, events // block),
        in_specs=[
            spread,
            pl.BlockSpec((1, targets, 1), lambda u, e: (u, 0, 0)),
            event_block,
            event_block,
        ],
        out_specs=[
            spread,
            pl.BlockSpec((1, heads, targets, block), lambda u, e: (u, 0, 0, e)),
        ],
        out_shape=[
            jax.ShapeDtypeStruct(queries.shape, BF16),
            jax.ShapeDtypeStruct((users, heads, targets, events), BF16),
        ],
        scratch_shapes=[
            pltpu.VMEM((targets, local), BF16),
            pltpu.VMEM((targets, local), F32),
        ],
        compiler_params=params("arbitrary", "arbitrary"),
        name="attention_forward",
    )(queries, limits, keys, values)


def norm_kernel(heads, parts_ref, gates_ref, og_ref, send_ref, gg_ref):
    total = parts_ref[0].astype(F32)
    for index in range(1, parts_ref.shape[0]):
        total = total + parts_ref[index].astype(F32)
    attended = total.reshape(gates_ref.shape)
    pieces = []
    for head in range(heads):
        lanes = slice(head * DH, (head + 1) * DH)
        rows = attended[:, lanes]
        rscale = lax.rsqrt(jnp.mean(rows * rows, axis=-1, keepdims=True) + 1e-06)
        normed = rows * rscale
        out_grad = og_ref[:, lanes]
        gg_ref[:, lanes] = out_grad * normed
        normed_grad = out_grad * gates_ref[:, lanes]
        mean = jnp.mean(normed_grad * normed, axis=-1, keepdims=True)
        pieces.append(rscale * (normed_grad - normed * mean))
    grad = jnp.concatenate(pieces, axis=-1)
    block = grad.reshape(send_ref.shape[1:]).astype(BF16)
    for index in range(send_ref.shape[0]):
        send_ref[index] = block


def norm_grads(partials, gates, out_grad, heads):
    return pl.pallas_call(
        functools.partial(norm_kernel, heads),
        out_shape=[
            jax.ShapeDtypeStruct(partials.shape, BF16),
            jax.ShapeDtypeStruct(gates.shape, F32),
        ],
        compiler_params=params(),
        name="norm_grads",
    )(partials, gates, out_grad)


def backward_kernel(scale, heads, grad_ref, slope_ref, key_ref, value_ref, out_ref, g_ref, acc_ref):
    step = pl.program_id(1)

    @pl.when(step == 0)
    def _():
        g_ref[...] = grad_ref[...].astype(F32).reshape(g_ref.shape).astype(BF16)
        acc_ref[...] = jnp.zeros_like(acc_ref)

    for head in range(heads):
        lanes = slice(head * DH, (head + 1) * DH)
        weight_grad = contract_last(g_ref[:, lanes], value_ref[0, :, lanes])
        grad_scores = (weight_grad * slope_ref[0, head].astype(F32)).astype(BF16)
        acc_ref[:, lanes] += matmul(grad_scores, key_ref[0, :, lanes])

    @pl.when(step == pl.num_programs(1) - 1)
    def _():
        out_ref[...] = (acc_ref[...] * scale).reshape(out_ref.shape).astype(BF16)


def backward_attention(grads, slopes, keys, values, heads, block):
    copies, users, rows, local = grads.shape
    events = keys.shape[1]
    targets = copies * rows
    spread = pl.BlockSpec((copies, 1, rows, local), lambda u, e: (0, u, 0, 0))
    event_block = pl.BlockSpec((1, block, local), lambda u, e: (u, e, 0))
    return pl.pallas_call(
        functools.partial(backward_kernel, DH ** (-0.5), heads),
        grid=(users, events // block),
        in_specs=[
            spread,
            pl.BlockSpec((1, heads, targets, block), lambda u, e: (u, 0, 0, e)),
            event_block,
            event_block,
        ],
        out_specs=spread,
        out_shape=jax.ShapeDtypeStruct(grads.shape, BF16),
        scratch_shapes=[
            pltpu.VMEM((targets, local), BF16),
            pltpu.VMEM((targets, local), F32),
        ],
        compiler_params=params("arbitrary", "arbitrary"),
        name="attention_backward",
    )(grads, slopes, keys, values)


def embed_kernel(parts_ref, gg_ref, qs_ref, gs_ref, wq_ref, wg_ref, out_ref):
    total = parts_ref[0].astype(F32)
    for index in range(1, parts_ref.shape[0]):
        total = total + parts_ref[index].astype(F32)
    query_back = (total.reshape(qs_ref.shape) * qs_ref[...]).astype(BF16)
    gate_back = (gg_ref[...] * gs_ref[...]).astype(BF16)
    out_ref[...] = contract_last(query_back, wq_ref[...]) + contract_last(gate_back, wg_ref[...])


def embed_grads(partials, gate_grad, query_slope, gate_slope, w_query, w_gate):
    return pl.pallas_call(
        embed_kernel,
        out_shape=jax.ShapeDtypeStruct((gate_grad.shape[0], w_query.shape[0]), F32),
        compiler_params=params(),
        name="embed_grads",
    )(partials, gate_grad, query_slope, gate_slope, w_query, w_gate)


def content_kernel(parts, mine_ref, other_ref, we_ref, slope_ref, wh_ref, head_ref, keep_ref, send_ref, back_ref):
    count = mine_ref.shape[0]
    half = back_ref.shape[0] // 2

    @pl.when(pl.program_id(0) == 0)
    def _():
        embed_grad = (0.5 * (mine_ref[...] + other_ref[...])).astype(BF16)
        hidden_grad = contract_last(embed_grad, we_ref[...])
        for index in range(parts):
            rows = slice(index * count, (index + 1) * count)
            back_ref[rows] = (hidden_grad * slope_ref[rows]).astype(BF16)

    head = head_ref[0]
    kept = pl.multiple_of(head * half, half)
    sent = pl.multiple_of((1 - head) * half, half)
    keep_ref[...] = contract_last(back_ref[pl.ds(kept, half), :], wh_ref[...])
    send_ref[...] = contract_last(back_ref[pl.ds(sent, half), :], wh_ref[...]).astype(BF16)


def content_grads(mine, other, w_embed, slopes, w_hidden, head, parts, block):
    count, hidden = slopes.shape
    width = w_hidden.shape[0]
    columns = pl.BlockSpec((count // 2, block), lambda j: (0, j))
    return pl.pallas_call(
        functools.partial(content_kernel, parts),
        grid=(width // block,),
        in_specs=[
            whole(mine.shape),
            whole(other.shape),
            whole(w_embed.shape),
            whole(slopes.shape),
            pl.BlockSpec((block, hidden), lambda j: (j, 0)),
            pl.BlockSpec(memory_space=pltpu.SMEM),
        ],
        out_specs=[columns, columns],
        out_shape=[
            jax.ShapeDtypeStruct((count // 2, width), F32),
            jax.ShapeDtypeStruct((count // 2, width), BF16),
        ],
        scratch_shapes=[pltpu.VMEM((count, hidden), BF16)],
        compiler_params=params("arbitrary"),
        name="content_grads",
    )(mine, other, w_embed, slopes, w_hidden, head)


def body(
    head_count,
    content_rows,
    w_hidden,
    w_embed,
    w_query,
    w_gate,
    w_proj,
    history_keys,
    history_values,
    cutoffs,
    out_cotangent,
):
    users, shard_rows, parts, width = content_rows.shape
    local = w_query.shape[1]
    heads = local // DH
    events = history_keys.shape[1]
    count = users * shard_rows
    copies = cutoffs.shape[1] // shard_rows
    swap = [(index, (index + 1) % head_count) for index in range(head_count)]
    head = lax.axis_index("head").astype(jnp.int32)

    def to_owner(blocks):
        return lax.all_to_all(blocks, "ctx", 0, 0, tiled=True)

    rows = content_rows.reshape(count, parts, width).transpose(1, 0, 2).reshape(-1, width)
    hidden_slope, mine = encode(rows, w_hidden, w_embed, parts, 512)
    other = lax.ppermute(mine, "head", swap)
    cotangent = out_cotangent.reshape(count, -1)
    sends, gates, out_grad, query_slope, gate_slope = project(
        mine, other, w_query, w_gate, w_proj, cotangent, copies, users
    )
    queries = to_owner(sends)
    limits = (cutoffs - lax.axis_index("ctx") * events)[:, :, None]
    block = events // 3
    partial, slopes = forward_attention(queries, limits, history_keys, history_values, heads, block)
    sends, gate_grad = norm_grads(to_owner(partial), gates, out_grad, heads)
    grads = to_owner(sends)
    partial = backward_attention(grads, slopes, history_keys, history_values, heads, block)
    mine = embed_grads(to_owner(partial), gate_grad, query_slope, gate_slope, w_query, w_gate)
    other = lax.ppermute(mine, "head", swap)
    keep, send = content_grads(
        mine, other, w_embed, hidden_slope, w_hidden, head[None], parts, 512
    )
    got = lax.ppermute(send, "head", swap)
    total = (keep + got.astype(F32)).astype(BF16)
    half = parts // head_count
    return total.reshape(half, count, width).transpose(1, 0, 2).reshape(users, shard_rows, half, width)


def solution(mesh):
    in_specs = (
        P(None, "ctx", None, None),
        P(None, "head"),
        P("head", None),
        P(None, "head"),
        P(None, "head"),
        P("head", None),
        P(None, "ctx", "head"),
        P(None, "ctx", "head"),
        P(),
        P(None, "ctx", None),
    )
    out_specs = P(None, "ctx", "head", None)
    return jax.shard_map(
        functools.partial(body, mesh.shape["head"]),
        mesh=mesh,
        in_specs=in_specs,
        out_specs=out_specs,
        check_vma=False,
    )
```

```python
import functools

import jax
import jax.numpy as jnp
from jax import lax
from jax.experimental import pallas as pl
from jax.experimental.pallas import tpu as pltpu
from jax.sharding import PartitionSpec as P

DH = 128
F32 = jnp.float32
BF16 = jnp.bfloat16


def matmul(left, right):
    return jnp.dot(left, right, preferred_element_type=F32)


def contract_last(left, right):
    return lax.dot_general(left, right, (((1,), (1,)), ((), ())), preferred_element_type=F32)


def silu_parts(half):
    tanh = jnp.tanh(half)
    lift = 1.0 + tanh
    value = half * lift
    return value, lift + value * (1.0 - tanh)


def params(mebibytes):
    return pltpu.CompilerParams(vmem_limit_bytes=mebibytes << 20)


def in_vmem(count):
    return [pl.BlockSpec(memory_space=pltpu.VMEM)] * count


def in_hbm(array):
    return pltpu.with_memory_space_constraint(array, pltpu.HBM)


def kept_in_vmem(array):
    return pltpu.with_memory_space_constraint(array, pltpu.VMEM)


def chunk_of(length, wanted):
    while length % wanted:
        wanted //= 2
    return wanted


def encode_kernel(parts, block, rows_ref, wh_hbm, we_hbm, slope_ref, out_ref, wh_ref, we_ref, rm_ref, sems):
    total_rows, hidden = slope_ref.shape
    blocks = hidden // block
    count = total_rows // parts
    copies = []
    for index in range(blocks):
        columns = pl.ds(index * block, block)
        copies.append(
            (
                pltpu.make_async_copy(wh_hbm.at[:, columns], wh_ref.at[:, columns], sems.at[0, index]),
                pltpu.make_async_copy(we_hbm.at[columns, :], we_ref.at[columns, :], sems.at[1, index]),
            )
        )
    for pair in copies:
        pair[0].start()
        pair[1].start()
    spot = lax.broadcasted_iota(jnp.int32, (total_rows, total_rows), 0)
    from_row = lax.broadcasted_iota(jnp.int32, (total_rows, total_rows), 1)
    wanted = (spot % count) * parts + spot // count
    order = jnp.where(from_row == wanted, 1.0, 0.0).astype(BF16)
    rows = rows_ref[...].astype(F32).reshape(total_rows, rows_ref.shape[2]).astype(BF16)
    rm_ref[...] = matmul(order, rows).astype(BF16)
    total = jnp.zeros((total_rows, we_ref.shape[1]), F32)
    for index in range(blocks):
        columns = slice(index * block, (index + 1) * block)
        copies[index][0].wait()
        lin = matmul(rm_ref[...], wh_ref[:, columns])
        value, slope = silu_parts(0.5 * lin)
        slope_ref[:, columns] = slope
        copies[index][1].wait()
        total = total + matmul(value.astype(BF16), we_ref[columns, :])
    summed = total[0:count]
    for part in range(1, parts):
        summed = summed + total[part * count : (part + 1) * count]
    out_ref[...] = summed


def encode(content, w_hidden, w_embed, block):
    count, parts, width = content.shape
    hidden = w_hidden.shape[1]
    model = w_embed.shape[1]
    return pl.pallas_call(
        functools.partial(encode_kernel, parts, block),
        in_specs=in_vmem(1) + [pl.BlockSpec(memory_space=pltpu.HBM)] * 2,
        out_specs=in_vmem(4),
        out_shape=[
            pltpu.VMEM((count * parts, hidden), F32),
            jax.ShapeDtypeStruct((count, model), F32),
            pltpu.VMEM(w_hidden.shape, BF16),
            pltpu.VMEM(w_embed.shape, BF16),
        ],
        scratch_shapes=[
            pltpu.VMEM((count * parts, width), BF16),
            pltpu.SemaphoreType.DMA((2, hidden // block)),
        ],
        compiler_params=params(16),
        name="encode",
    )(content, in_hbm(w_hidden), in_hbm(w_embed))


def project_kernel(
    mine_ref, other_ref, wq_ref, wg_ref, wp_ref, cot_ref, send_ref, gates_ref, og_ref, qs_ref, gs_ref
):
    embedded = (0.5 * (mine_ref[...] + other_ref[...])).astype(BF16)
    query, query_slope = silu_parts(0.5 * matmul(embedded, wq_ref[...]))
    gate, gate_slope = silu_parts(0.5 * matmul(embedded, wg_ref[...]))
    qs_ref[...] = 0.5 * query_slope
    gs_ref[...] = 0.5 * gate_slope
    gates_ref[...] = gate.astype(BF16).astype(F32)
    og_ref[...] = contract_last(cot_ref[...], wp_ref[...]).astype(BF16).astype(F32)
    block = query.reshape(send_ref.shape[1:]).astype(BF16)
    for index in range(send_ref.shape[0]):
        send_ref[index] = block


def project(mine, other, w_query, w_gate, w_proj, cotangent, copies, users):
    count = mine.shape[0]
    local = w_query.shape[1]
    rows = jax.ShapeDtypeStruct((count, local), F32)
    return pl.pallas_call(
        project_kernel,
        out_shape=[jax.ShapeDtypeStruct((copies, users, count // users, local), BF16)] + [rows] * 4,
        compiler_params=params(8),
        name="project",
    )(mine, other, w_query, w_gate, w_proj, cotangent)


def forward_kernel(
    scale,
    heads,
    block,
    query_ref,
    cutoff_ref,
    key_hbm,
    value_hbm,
    out_ref,
    slope_ref,
    key_ref,
    value_ref,
    limit_ref,
    sems,
):
    users, events = key_ref.shape[0], key_ref.shape[1]
    base = lax.axis_index("ctx") * events

    def fetch(user):
        return (
            pltpu.make_async_copy(key_hbm.at[user], key_ref.at[user], sems.at[0, user]),
            pltpu.make_async_copy(value_hbm.at[user], value_ref.at[user], sems.at[1, user]),
        )

    for user in range(min(2, users)):
        for copy in fetch(user):
            copy.start()
    targets, local = query_ref.shape[0] * query_ref.shape[2], query_ref.shape[3]
    half_scale = jnp.asarray(0.5 * scale, F32)
    spots = lax.broadcasted_iota(jnp.int32, (targets, block), 1).astype(F32).astype(BF16)

    def one_user(user, carry):
        queries = query_ref[:, pl.ds(user, 1)].astype(F32).reshape(targets, local).astype(BF16)
        limits = (cutoff_ref[pl.ds(user, 1), :] - base).astype(F32)
        limit_ref[...] = jnp.broadcast_to(limits, (targets, targets)).T

        @pl.when(user + 2 < users)
        def _():
            for copy in fetch(user + 2):
                copy.start()

        for copy in fetch(user):
            copy.wait()
        totals = [jnp.zeros((targets, DH), F32) for _ in range(heads)]
        for start in range(0, events, block):
            rows = slice(start, start + block)
            left = jnp.broadcast_to(limit_ref[:, 0:1] - float(start), (targets, block)).astype(BF16)
            visible = spots < left
            for head in range(heads):
                lanes = slice(head * DH, (head + 1) * DH)
                raw = contract_last(queries[:, lanes], key_ref[user, rows, lanes])
                half = (raw * half_scale).astype(BF16)
                tanh = jnp.where(visible, jnp.tanh(half), jnp.asarray(-1.0, BF16))
                lift = jnp.asarray(1.0, BF16) + tanh
                weights = half * lift
                slope_ref[user, head, :, rows] = lift + weights * (jnp.asarray(1.0, BF16) - tanh)
                totals[head] = totals[head] + matmul(weights, value_ref[user, rows, lanes])
        total = jnp.concatenate(totals, axis=-1)
        out_ref[:, pl.ds(user, 1)] = total.reshape(-1, 1, query_ref.shape[2], local).astype(BF16)
        return carry

    lax.fori_loop(0, users, one_user, 0)


def forward_attention(queries, cutoffs, keys, values, heads):
    copies, users, rows, local = queries.shape
    events = keys.shape[1]
    targets = copies * rows
    return pl.pallas_call(
        functools.partial(forward_kernel, DH ** (-0.5), heads, chunk_of(events, 256)),
        in_specs=in_vmem(2) + [pl.BlockSpec(memory_space=pltpu.HBM)] * 2,
        out_specs=in_vmem(4),
        out_shape=[
            jax.ShapeDtypeStruct(queries.shape, BF16),
            pltpu.VMEM((users, heads, targets, events), BF16),
            pltpu.VMEM(keys.shape, BF16),
            pltpu.VMEM(values.shape, BF16),
        ],
        scratch_shapes=[
            pltpu.VMEM((targets, targets), F32),
            pltpu.SemaphoreType.DMA((2, users)),
        ],
        compiler_params=params(16),
        name="attention_forward",
    )(queries, cutoffs, in_hbm(keys), in_hbm(values))


def norm_kernel(heads, parts_ref, gates_ref, og_ref, send_ref, gg_ref):
    total = parts_ref[0].astype(F32)
    for index in range(1, parts_ref.shape[0]):
        total = total + parts_ref[index].astype(F32)
    attended = total.reshape(gates_ref.shape)
    pieces = []
    for head in range(heads):
        lanes = slice(head * DH, (head + 1) * DH)
        rows = attended[:, lanes]
        rscale = lax.rsqrt(jnp.mean(rows * rows, axis=-1, keepdims=True) + 1e-06)
        normed = rows * rscale
        out_grad = og_ref[:, lanes]
        gg_ref[:, lanes] = out_grad * normed
        normed_grad = out_grad * gates_ref[:, lanes]
        mean = jnp.mean(normed_grad * normed, axis=-1, keepdims=True)
        pieces.append(rscale * (normed_grad - normed * mean))
    grad = jnp.concatenate(pieces, axis=-1)
    block = grad.reshape(send_ref.shape[1:]).astype(BF16)
    for index in range(send_ref.shape[0]):
        send_ref[index] = block


def norm_grads(partials, gates, out_grad, heads):
    return pl.pallas_call(
        functools.partial(norm_kernel, heads),
        out_shape=[
            jax.ShapeDtypeStruct(partials.shape, BF16),
            jax.ShapeDtypeStruct(gates.shape, F32),
        ],
        compiler_params=params(8),
        name="norm_grads",
    )(partials, gates, out_grad)


def backward_kernel(scale, heads, block, grad_ref, slope_ref, key_ref, value_ref, out_ref):
    users, events = key_ref.shape[0], key_ref.shape[1]
    targets, local = grad_ref.shape[0] * grad_ref.shape[2], grad_ref.shape[3]

    def one_user(user, carry):
        grads = grad_ref[:, pl.ds(user, 1)].astype(F32).reshape(targets, local).astype(BF16)
        totals = [jnp.zeros((targets, DH), F32) for _ in range(heads)]
        for start in range(0, events, block):
            rows = slice(start, start + block)
            for head in range(heads):
                lanes = slice(head * DH, (head + 1) * DH)
                weight_grad = contract_last(grads[:, lanes], value_ref[user, rows, lanes])
                grad_scores = weight_grad.astype(BF16) * slope_ref[user, head, :, rows]
                totals[head] = totals[head] + matmul(grad_scores, key_ref[user, rows, lanes])
        total = jnp.concatenate(totals, axis=-1) * (0.5 * scale)
        out_ref[:, pl.ds(user, 1)] = total.reshape(-1, 1, grad_ref.shape[2], local).astype(BF16)
        return carry

    lax.fori_loop(0, users, one_user, 0)


def backward_attention(grads, slopes, keys, values, heads):
    return pl.pallas_call(
        functools.partial(backward_kernel, DH ** (-0.5), heads, chunk_of(keys.shape[1], 256)),
        in_specs=in_vmem(4),
        out_specs=in_vmem(1)[0],
        out_shape=jax.ShapeDtypeStruct(grads.shape, BF16),
        compiler_params=params(16),
        name="attention_backward",
    )(grads, kept_in_vmem(slopes), kept_in_vmem(keys), kept_in_vmem(values))


def embed_kernel(parts_ref, gg_ref, qs_ref, gs_ref, wq_ref, wg_ref, out_ref):
    total = parts_ref[0].astype(F32)
    for index in range(1, parts_ref.shape[0]):
        total = total + parts_ref[index].astype(F32)
    query_back = (total.reshape(qs_ref.shape) * qs_ref[...]).astype(BF16)
    gate_back = (gg_ref[...] * gs_ref[...]).astype(BF16)
    out_ref[...] = contract_last(query_back, wq_ref[...]) + contract_last(gate_back, wg_ref[...])


def embed_grads(partials, gate_grad, query_slope, gate_slope, w_query, w_gate):
    return pl.pallas_call(
        embed_kernel,
        out_shape=jax.ShapeDtypeStruct((gate_grad.shape[0], w_query.shape[0]), F32),
        compiler_params=params(8),
        name="embed_grads",
    )(partials, gate_grad, query_slope, gate_slope, w_query, w_gate)


def content_kernel(parts, block, mine_ref, other_ref, we_ref, slope_ref, wh_ref, keep_ref, send_ref, back_ref):
    count = mine_ref.shape[0]
    half = parts // 2
    kept = half * count
    embed_grad = (0.5 * (mine_ref[...] + other_ref[...])).astype(BF16)
    hidden_grad = 0.5 * contract_last(embed_grad, we_ref[...])
    head = lax.axis_index("head")
    for index in range(parts):
        side = head if index < half else 1 - head
        source = pl.multiple_of((side * half + index % half) * count, count)
        back_ref[index * count : (index + 1) * count] = (
            hidden_grad * slope_ref[pl.ds(source, count), :]
        ).astype(BF16)
    for start in range(0, wh_ref.shape[0], block):
        columns = slice(start, start + block)
        part = contract_last(back_ref[...], wh_ref[columns, :])
        keep_ref[:, columns] = part[:kept]
        send_ref[:, columns] = part[kept:].astype(BF16)


def content_grads(mine, other, w_embed, slopes, w_hidden, parts, block):
    count, hidden = slopes.shape
    width = w_hidden.shape[0]
    return pl.pallas_call(
        functools.partial(content_kernel, parts, block),
        in_specs=in_vmem(5),
        out_specs=in_vmem(2),
        out_shape=[
            jax.ShapeDtypeStruct((count // 2, width), F32),
            jax.ShapeDtypeStruct((count // 2, width), BF16),
        ],
        scratch_shapes=[pltpu.VMEM((count, hidden), BF16)],
        compiler_params=params(16),
        name="content_grads",
    )(mine, other, kept_in_vmem(w_embed), kept_in_vmem(slopes), kept_in_vmem(w_hidden))


def body(
    head_count,
    content_rows,
    w_hidden,
    w_embed,
    w_query,
    w_gate,
    w_proj,
    history_keys,
    history_values,
    cutoffs,
    out_cotangent,
):
    users, shard_rows, parts, width = content_rows.shape
    local = w_query.shape[1]
    heads = local // DH
    count = users * shard_rows
    copies = cutoffs.shape[1] // shard_rows
    swap = [(index, (index + 1) % head_count) for index in range(head_count)]

    def to_owner(blocks):
        return lax.all_to_all(blocks, "ctx", 0, 0, tiled=True)

    hidden_slope, mine, w_hidden, w_embed = encode(
        content_rows.reshape(count, parts, width), w_hidden, w_embed, 256
    )
    other = lax.ppermute(mine, "head", swap)
    cotangent = out_cotangent.reshape(count, -1)
    sends, gates, out_grad, query_slope, gate_slope = project(
        mine, other, w_query, w_gate, w_proj, cotangent, copies, users
    )
    queries = to_owner(sends)
    partial, slopes, history_keys, history_values = forward_attention(
        queries, cutoffs, history_keys, history_values, heads
    )
    sends, gate_grad = norm_grads(to_owner(partial), gates, out_grad, heads)
    grads = to_owner(sends)
    partial = backward_attention(grads, slopes, history_keys, history_values, heads)
    mine = embed_grads(to_owner(partial), gate_grad, query_slope, gate_slope, w_query, w_gate)
    other = lax.ppermute(mine, "head", swap)
    keep, send = content_grads(
        mine, other, w_embed, hidden_slope, w_hidden, parts, 256
    )
    got = lax.ppermute(send, "head", swap)
    total = (keep + got.astype(F32)).astype(BF16)
    half = parts // head_count
    return total.reshape(half, count, width).transpose(1, 0, 2).reshape(users, shard_rows, half, width)


def solution(mesh):
    in_specs = (
        P(None, "ctx", None, None),
        P(None, "head"),
        P("head", None),
        P(None, "head"),
        P(None, "head"),
        P("head", None),
        P(None, "ctx", "head"),
        P(None, "ctx", "head"),
        P(),
        P(None, "ctx", None),
    )
    out_specs = P(None, "ctx", "head", None)
    return jax.shard_map(
        functools.partial(body, mesh.shape["head"]),
        mesh=mesh,
        in_specs=in_specs,
        out_specs=out_specs,
        check_vma=False,
    )
```

```python
import functools

import jax
import jax.numpy as jnp
from jax import lax
from jax.experimental import pallas as pl
from jax.experimental.pallas import tpu as pltpu
from jax.sharding import PartitionSpec as P


DH = 128
F32 = jnp.float32
BF16 = jnp.bfloat16
GROUP = 9


def matmul(left, right):
    return jnp.dot(left, right, preferred_element_type=F32)


def contract_last(left, right):
    return lax.dot_general(left, right, (((1,), (1,)), ((), ())), preferred_element_type=F32)


def silu_parts(half):
    tanh = jnp.tanh(half)
    lift = 1.0 + tanh
    value = half * lift
    return value, lift + value * (1.0 - tanh)


def params(mebibytes):
    return pltpu.CompilerParams(vmem_limit_bytes=mebibytes << 20)


def in_vmem(count):
    return [pl.BlockSpec(memory_space=pltpu.VMEM)] * count


def in_hbm(array):
    return pltpu.with_memory_space_constraint(array, pltpu.HBM)


def kept_in_vmem(array):
    return pltpu.with_memory_space_constraint(array, pltpu.VMEM)


def chunks_of(length):
    block = 256
    while length % block:
        block //= 2
    group = GROUP
    while (length // block) % group:
        group -= 1
    return block, group


def encode_kernel(
    parts, block, depth, rows_hbm, wh_hbm, we_hbm, slope_ref, out_ref, wh_ref, we_ref, rows_ref, rm_ref, sems, row_sem
):
    total_rows, hidden = slope_ref.shape
    blocks = hidden // block
    count = total_rows // parts
    copies = []
    for index in range(blocks):
        columns = pl.ds(index * block, block)
        copies.append(
            (
                pltpu.make_async_copy(wh_hbm.at[:, columns], wh_ref.at[:, columns], sems.at[0, index]),
                pltpu.make_async_copy(we_hbm.at[columns, :], we_ref.at[columns, :], sems.at[1, index]),
            )
        )
    rows_copy = pltpu.make_async_copy(rows_hbm, rows_ref, row_sem)
    rows_copy.start()
    for pair in copies[:depth]:
        pair[0].start()
        pair[1].start()
    spot = lax.broadcasted_iota(jnp.int32, (total_rows, total_rows), 0)
    from_row = lax.broadcasted_iota(jnp.int32, (total_rows, total_rows), 1)
    wanted = (spot % count) * parts + spot // count
    order = jnp.where(from_row == wanted, 1.0, 0.0).astype(BF16)
    rows_copy.wait()
    rows = rows_ref[...].astype(F32).reshape(total_rows, rows_ref.shape[2]).astype(BF16)
    rm_ref[...] = matmul(order, rows).astype(BF16)
    total = jnp.zeros((total_rows, we_ref.shape[1]), F32)
    for index in range(blocks):
        columns = slice(index * block, (index + 1) * block)
        if index + depth < blocks:
            copies[index + depth][0].start()
            copies[index + depth][1].start()
        copies[index][0].wait()
        lin = matmul(rm_ref[...], wh_ref[:, columns])
        value, slope = silu_parts(0.5 * lin)
        slope_ref[:, columns] = slope
        copies[index][1].wait()
        total = total + matmul(value.astype(BF16), we_ref[columns, :])
    summed = total[0:count]
    for part in range(1, parts):
        summed = summed + total[part * count : (part + 1) * count]
    out_ref[...] = summed


def encode(content, w_hidden, w_embed, block):
    count, parts, width = content.shape
    hidden = w_hidden.shape[1]
    model = w_embed.shape[1]
    return pl.pallas_call(
        functools.partial(encode_kernel, parts, block, 3),
        in_specs=[pl.BlockSpec(memory_space=pltpu.HBM)] * 3,
        out_specs=in_vmem(4),
        out_shape=[
            pltpu.VMEM((count * parts, hidden), F32),
            jax.ShapeDtypeStruct((count, model), F32),
            pltpu.VMEM(w_hidden.shape, BF16),
            pltpu.VMEM(w_embed.shape, BF16),
        ],
        scratch_shapes=[
            pltpu.VMEM(content.shape, BF16),
            pltpu.VMEM((count * parts, width), BF16),
            pltpu.SemaphoreType.DMA((2, hidden // block)),
            pltpu.SemaphoreType.DMA,
        ],
        compiler_params=params(16),
        name="encode",
    )(in_hbm(content), in_hbm(w_hidden), in_hbm(w_embed))


def warm_kernel(after_ref, cot_ref, wp_ref, key_hbm, value_hbm, og_ref, key_ref, value_ref, sems):
    copies = (
        pltpu.make_async_copy(key_hbm.at[0], key_ref, sems.at[0]),
        pltpu.make_async_copy(value_hbm.at[0], value_ref, sems.at[1]),
    )
    for copy in copies:
        copy.start()
    og_ref[...] = contract_last(cot_ref[...], wp_ref[...]).astype(BF16).astype(F32)
    for copy in copies:
        copy.wait()


def warm(after, cotangent, w_proj, keys, values):
    return pl.pallas_call(
        warm_kernel,
        in_specs=in_vmem(3) + [pl.BlockSpec(memory_space=pltpu.HBM)] * 2,
        out_specs=in_vmem(3),
        out_shape=[
            jax.ShapeDtypeStruct((cotangent.shape[0], w_proj.shape[0]), F32),
            pltpu.VMEM(keys.shape[1:], BF16),
            pltpu.VMEM(values.shape[1:], BF16),
        ],
        scratch_shapes=[pltpu.SemaphoreType.DMA((2,))],
        compiler_params=params(8),
        name="warm",
    )(after, cotangent, w_proj, in_hbm(keys), in_hbm(values))


def project_kernel(mine_ref, other_ref, wq_ref, wg_ref, og_ref, send_ref, ng_ref, qs_ref, gs_ref):
    embedded = (0.5 * (mine_ref[...] + other_ref[...])).astype(BF16)
    query, query_slope = silu_parts(0.5 * matmul(embedded, wq_ref[...]))
    gate, gate_slope = silu_parts(0.5 * matmul(embedded, wg_ref[...]))
    qs_ref[...] = 0.5 * query_slope
    gs_ref[...] = 0.5 * gate_slope
    ng_ref[...] = og_ref[...] * gate.astype(BF16).astype(F32)
    block = (query * (0.5 * DH ** (-0.5))).reshape(send_ref.shape[1:]).astype(BF16)
    for index in range(send_ref.shape[0]):
        send_ref[index] = block


def project(mine, other, w_query, w_gate, out_grad, copies, users):
    count = mine.shape[0]
    local = w_query.shape[1]
    rows = jax.ShapeDtypeStruct((count, local), F32)
    return pl.pallas_call(
        project_kernel,
        out_shape=[jax.ShapeDtypeStruct((copies, users, count // users, local), BF16)] + [rows] * 3,
        compiler_params=params(8),
        name="project",
    )(mine, other, w_query, w_gate, out_grad)


def forward_kernel(
    heads,
    block,
    group,
    query_ref,
    cutoff_ref,
    first_key_ref,
    first_value_ref,
    key_hbm,
    value_hbm,
    out_ref,
    slope_ref,
    key_ref,
    value_ref,
    limit_ref,
    sems,
):
    users, events = key_hbm.shape[0], key_hbm.shape[1]
    base = lax.axis_index("ctx") * events

    def fetch(user):
        return (
            pltpu.make_async_copy(key_hbm.at[user], key_ref.at[user - 1], sems.at[0, user - 1]),
            pltpu.make_async_copy(value_hbm.at[user], value_ref.at[user - 1], sems.at[1, user - 1]),
        )

    for user in range(1, min(3, users)):
        for copy in fetch(user):
            copy.start()
    targets, local = query_ref.shape[0] * query_ref.shape[2], query_ref.shape[3]
    one = jnp.asarray(1.0, BF16)
    spots = lax.broadcasted_iota(jnp.int32, (targets, block), 1).astype(F32).astype(BF16)

    for user in range(users):
        queries = query_ref[:, pl.ds(user, 1)].astype(F32).reshape(targets, local).astype(BF16)
        limits = (cutoff_ref[pl.ds(user, 1), :] - base).astype(F32)
        limit_ref[...] = jnp.broadcast_to(limits, (block, targets)).T

        if user == 0:
            keys_here, values_here = first_key_ref, first_value_ref
        else:
            if user + 2 < users:
                for copy in fetch(user + 2):
                    copy.start()
            for copy in fetch(user):
                copy.wait()
            keys_here, values_here = key_ref.at[user - 1], value_ref.at[user - 1]
        totals = [jnp.zeros((targets, DH), F32) for _ in range(heads)]
        for first in range(0, events, block * group):
            span = slice(first, first + block * group)
            for head in range(heads):
                lanes = slice(head * DH, (head + 1) * DH)
                weights = []
                for start in range(first, first + block * group, block):
                    rows = slice(start, start + block)
                    left = (limit_ref[...] - float(start)).astype(BF16)
                    visible = spots < left
                    half = contract_last(queries[:, lanes], keys_here[rows, lanes]).astype(BF16)
                    tanh = jnp.where(visible, jnp.tanh(half), -one)
                    lift = one + tanh
                    weight = half * lift
                    slope_ref[user, head, :, rows] = lift + weight * (one - tanh)
                    weights.append(weight)
                totals[head] = totals[head] + matmul(
                    jnp.concatenate(weights, axis=-1), values_here[span, lanes]
                )
        total = jnp.concatenate(totals, axis=-1)
        out_ref[:, pl.ds(user, 1)] = total.reshape(-1, 1, query_ref.shape[2], local).astype(BF16)


def forward_attention(queries, cutoffs, first_keys, first_values, keys, values, heads):
    copies, users, rows, _ = queries.shape
    events = keys.shape[1]
    targets = copies * rows
    return pl.pallas_call(
        functools.partial(forward_kernel, heads, *chunks_of(events)),
        in_specs=in_vmem(4) + [pl.BlockSpec(memory_space=pltpu.HBM)] * 2,
        out_specs=in_vmem(4),
        out_shape=[
            jax.ShapeDtypeStruct(queries.shape, BF16),
            pltpu.VMEM((users, heads, targets, events), BF16),
            pltpu.VMEM((users - 1,) + keys.shape[1:], BF16),
            pltpu.VMEM((users - 1,) + values.shape[1:], BF16),
        ],
        scratch_shapes=[
            pltpu.VMEM((targets, chunks_of(events)[0]), F32),
            pltpu.SemaphoreType.DMA((2, users - 1)),
        ],
        compiler_params=params(16),
        name="attention_forward",
    )(
        queries,
        cutoffs,
        kept_in_vmem(first_keys),
        kept_in_vmem(first_values),
        in_hbm(keys),
        in_hbm(values),
    )


def norm_kernel(heads, parts_ref, ng_ref, og_ref, send_ref, gg_ref):
    total = parts_ref[0].astype(F32)
    for index in range(1, parts_ref.shape[0]):
        total = total + parts_ref[index].astype(F32)
    attended = total.reshape(ng_ref.shape)
    pieces = []
    for head in range(heads):
        lanes = slice(head * DH, (head + 1) * DH)
        rows = attended[:, lanes]
        rscale = lax.rsqrt(jnp.mean(rows * rows, axis=-1, keepdims=True) + 1e-06)
        normed = rows * rscale
        gg_ref[:, lanes] = og_ref[:, lanes] * normed
        normed_grad = ng_ref[:, lanes]
        mean = jnp.mean(normed_grad * normed, axis=-1, keepdims=True)
        pieces.append(rscale * (normed_grad - normed * mean))
    grad = jnp.concatenate(pieces, axis=-1)
    block = grad.reshape(send_ref.shape[1:]).astype(BF16)
    for index in range(send_ref.shape[0]):
        send_ref[index] = block


def norm_grads(partials, normed_grad, out_grad, heads):
    return pl.pallas_call(
        functools.partial(norm_kernel, heads),
        out_shape=[
            jax.ShapeDtypeStruct(partials.shape, BF16),
            jax.ShapeDtypeStruct(out_grad.shape, F32),
        ],
        compiler_params=params(8),
        name="norm_grads",
    )(partials, normed_grad, out_grad)


def backward_kernel(
    scale, heads, block, group, grad_ref, slope_ref, first_key_ref, first_value_ref, key_ref, value_ref, out_ref
):
    users, events = grad_ref.shape[1], key_ref.shape[1]
    targets, local = grad_ref.shape[0] * grad_ref.shape[2], grad_ref.shape[3]

    for user in range(users):
        if user == 0:
            keys_here, values_here = first_key_ref, first_value_ref
        else:
            keys_here, values_here = key_ref.at[user - 1], value_ref.at[user - 1]
        grads = grad_ref[:, pl.ds(user, 1)].astype(F32).reshape(targets, local).astype(BF16)
        totals = [jnp.zeros((targets, DH), F32) for _ in range(heads)]
        for first in range(0, events, block * group):
            span = slice(first, first + block * group)
            for head in range(heads):
                lanes = slice(head * DH, (head + 1) * DH)
                scored = []
                for start in range(first, first + block * group, block):
                    rows = slice(start, start + block)
                    weight_grad = contract_last(grads[:, lanes], values_here[rows, lanes])
                    scored.append(weight_grad.astype(BF16) * slope_ref[user, head, :, rows])
                totals[head] = totals[head] + matmul(
                    jnp.concatenate(scored, axis=-1), keys_here[span, lanes]
                )
        total = jnp.concatenate(totals, axis=-1) * (0.5 * scale)
        out_ref[:, pl.ds(user, 1)] = total.reshape(-1, 1, grad_ref.shape[2], local).astype(BF16)


def backward_attention(grads, slopes, history, heads):
    return pl.pallas_call(
        functools.partial(backward_kernel, DH ** (-0.5), heads, *chunks_of(slopes.shape[3])),
        in_specs=in_vmem(6),
        out_specs=in_vmem(1)[0],
        out_shape=jax.ShapeDtypeStruct(grads.shape, BF16),
        compiler_params=params(16),
        name="attention_backward",
    )(grads, kept_in_vmem(slopes), *map(kept_in_vmem, history))


def embed_kernel(parts_ref, gg_ref, qs_ref, gs_ref, wq_ref, wg_ref, out_ref):
    total = parts_ref[0].astype(F32)
    for index in range(1, parts_ref.shape[0]):
        total = total + parts_ref[index].astype(F32)
    query_back = (total.reshape(qs_ref.shape) * qs_ref[...]).astype(BF16)
    gate_back = (gg_ref[...] * gs_ref[...]).astype(BF16)
    out_ref[...] = contract_last(query_back, wq_ref[...]) + contract_last(gate_back, wg_ref[...])


def embed_grads(partials, gate_grad, query_slope, gate_slope, w_query, w_gate):
    return pl.pallas_call(
        embed_kernel,
        out_shape=jax.ShapeDtypeStruct((gate_grad.shape[0], w_query.shape[0]), F32),
        compiler_params=params(8),
        name="embed_grads",
    )(partials, gate_grad, query_slope, gate_slope, w_query, w_gate)


def content_first_kernel(parts, block, mine_ref, other_ref, we_ref, slope_ref, wh_ref, keep_ref, send_ref, back_ref):
    count = mine_ref.shape[0]
    half = parts // 2
    embed_grad = (0.5 * (mine_ref[...] + other_ref[...])).astype(BF16)
    hidden_grad = 0.5 * contract_last(embed_grad, we_ref[...])
    head = lax.axis_index("head")
    for index in range(parts):
        side = head if index < half else 1 - head
        source = pl.multiple_of((side * half + index % half) * count, count)
        back_ref[index * count : (index + 1) * count] = (
            hidden_grad * slope_ref[pl.ds(source, count), :]
        ).astype(BF16)
    content_columns(0, block, back_ref, wh_ref, keep_ref, send_ref)


def content_columns(first, block, back_ref, wh_ref, keep_ref, send_ref):
    kept, width = keep_ref.shape
    for start in range(0, width, block):
        columns = slice(start, start + block)
        part = contract_last(back_ref[...], wh_ref[first + start : first + start + block, :])
        keep_ref[:, columns] = part[:kept]
        send_ref[:, columns] = part[kept:].astype(BF16)


def content_second_kernel(block, back_ref, wh_ref, keep_ref, send_ref):
    content_columns(wh_ref.shape[0] // 2, block, back_ref, wh_ref, keep_ref, send_ref)


def content_first(mine, other, w_embed, slopes, w_hidden, parts, block):
    count, hidden = slopes.shape
    shape = (count // 2, w_hidden.shape[0] // 2)
    return pl.pallas_call(
        functools.partial(content_first_kernel, parts, block),
        in_specs=in_vmem(5),
        out_specs=in_vmem(3),
        out_shape=[
            jax.ShapeDtypeStruct(shape, F32),
            jax.ShapeDtypeStruct(shape, BF16),
            pltpu.VMEM((count, hidden), BF16),
        ],
        compiler_params=params(16),
        name="content_first",
    )(mine, other, kept_in_vmem(w_embed), kept_in_vmem(slopes), kept_in_vmem(w_hidden))


def content_second(back, w_hidden, block):
    shape = (back.shape[0] // 2, w_hidden.shape[0] // 2)
    return pl.pallas_call(
        functools.partial(content_second_kernel, block),
        in_specs=in_vmem(2),
        out_specs=in_vmem(2),
        out_shape=[
            jax.ShapeDtypeStruct(shape, F32),
            jax.ShapeDtypeStruct(shape, BF16),
        ],
        compiler_params=params(16),
        name="content_second",
    )(kept_in_vmem(back), kept_in_vmem(w_hidden))


def combine_kernel(keep1_ref, got1_ref, keep2_ref, got2_ref, out_ref):
    count, half, width = out_ref.shape
    rows = count * half
    spot = lax.broadcasted_iota(jnp.int32, (rows, rows), 0)
    from_row = lax.broadcasted_iota(jnp.int32, (rows, rows), 1)
    order = jnp.where(from_row == (spot % half) * count + spot // half, 1.0, 0.0).astype(BF16)
    for first, keep_ref, got_ref in ((0, keep1_ref, got1_ref), (width // 2, keep2_ref, got2_ref)):
        total = (keep_ref[...] + got_ref[...].astype(F32)).astype(BF16)
        placed = matmul(order, total).reshape(count, half, width // 2)
        out_ref[:, :, first : first + width // 2] = placed.astype(BF16)


def combine(pieces, count, half, width):
    return pl.pallas_call(
        combine_kernel,
        in_specs=in_vmem(4),
        out_specs=in_vmem(1)[0],
        out_shape=jax.ShapeDtypeStruct((count, half, width), BF16),
        compiler_params=params(8),
        name="combine",
    )(*pieces)


def body(
    head_count,
    content_rows,
    w_hidden,
    w_embed,
    w_query,
    w_gate,
    w_proj,
    history_keys,
    history_values,
    cutoffs,
    out_cotangent,
):
    users, shard_rows, parts, width = content_rows.shape
    local = w_query.shape[1]
    heads = local // DH
    count = users * shard_rows
    copies = cutoffs.shape[1] // shard_rows
    swap = [(index, (index + 1) % head_count) for index in range(head_count)]

    def to_owner(blocks):
        return lax.all_to_all(blocks, "ctx", 0, 0, tiled=True)

    hidden_slope, mine, w_hidden, w_embed = encode(
        content_rows.reshape(count, parts, width), w_hidden, w_embed, 256
    )
    other = lax.ppermute(mine, "head", swap)
    cotangent = out_cotangent.reshape(count, -1)
    out_grad, first_keys, first_values = warm(mine, cotangent, w_proj, history_keys, history_values)
    sends, normed_grad, query_slope, gate_slope = project(
        mine, other, w_query, w_gate, out_grad, copies, users
    )
    partial, slopes, rest_keys, rest_values = forward_attention(
        to_owner(sends), cutoffs, first_keys, first_values, history_keys, history_values, heads
    )
    sends, gate_grad = norm_grads(to_owner(partial), normed_grad, out_grad, heads)
    history = (first_keys, first_values, rest_keys, rest_values)
    partial = backward_attention(to_owner(sends), slopes, history, heads)
    mine = embed_grads(to_owner(partial), gate_grad, query_slope, gate_slope, w_query, w_gate)
    other = lax.ppermute(mine, "head", swap)
    keep1, send1, back = content_first(mine, other, w_embed, hidden_slope, w_hidden, parts, 256)
    got1 = lax.ppermute(send1, "head", swap)
    keep2, send2 = content_second(back, w_hidden, 256)
    got2 = lax.ppermute(send2, "head", swap)
    half = parts // head_count
    total = combine((keep1, got1, keep2, got2), count, half, width)
    return total.reshape(users, shard_rows, half, width)


def solution(mesh):
    in_specs = (
        P(None, "ctx", None, None),
        P(None, "head"),
        P("head", None),
        P(None, "head"),
        P(None, "head"),
        P("head", None),
        P(None, "ctx", "head"),
        P(None, "ctx", "head"),
        P(),
        P(None, "ctx", None),
    )
    out_specs = P(None, "ctx", "head", None)
    return jax.shard_map(
        functools.partial(body, mesh.shape["head"]),
        mesh=mesh,
        in_specs=in_specs,
        out_specs=out_specs,
        check_vma=False,
    )
```

```python
import functools

import jax
import jax.numpy as jnp
from jax import lax
from jax.experimental import pallas as pl
from jax.experimental.pallas import tpu as pltpu
from jax.sharding import PartitionSpec as P


DH = 128
F32 = jnp.float32
BF16 = jnp.bfloat16
GROUP = 9


def matmul(left, right):
    return jnp.dot(left, right, preferred_element_type=F32)


def contract_last(left, right):
    return lax.dot_general(left, right, (((1,), (1,)), ((), ())), preferred_element_type=F32)


def silu_parts(half):
    tanh = jnp.tanh(half)
    lift = 1.0 + tanh
    value = half * lift
    return value, lift + value * (1.0 - tanh)


def params(mebibytes):
    return pltpu.CompilerParams(vmem_limit_bytes=mebibytes << 20)


def in_vmem(count):
    return [pl.BlockSpec(memory_space=pltpu.VMEM)] * count


def in_hbm(array):
    return pltpu.with_memory_space_constraint(array, pltpu.HBM)


def kept_in_vmem(array):
    return pltpu.with_memory_space_constraint(array, pltpu.VMEM)


def chunks_of(length):
    block = 256
    while length % block:
        block //= 2
    group = GROUP
    while (length // block) % group:
        group -= 1
    return block, group


def encode_kernel(
    parts, block, depth, rows_hbm, wh_hbm, we_hbm, slope_ref, out_ref, wh_ref, we_ref, rows_ref, rm_ref, sems, row_sem
):
    total_rows, hidden = slope_ref.shape
    blocks = hidden // block
    count = total_rows // parts
    copies = []
    for index in range(blocks):
        columns = pl.ds(index * block, block)
        copies.append(
            (
                pltpu.make_async_copy(wh_hbm.at[:, columns], wh_ref.at[:, columns], sems.at[0, index]),
                pltpu.make_async_copy(we_hbm.at[columns, :], we_ref.at[columns, :], sems.at[1, index]),
            )
        )
    rows_copy = pltpu.make_async_copy(rows_hbm, rows_ref, row_sem)
    rows_copy.start()
    for pair in copies[:depth]:
        pair[0].start()
        pair[1].start()
    spot = lax.broadcasted_iota(jnp.int32, (total_rows, total_rows), 0)
    from_row = lax.broadcasted_iota(jnp.int32, (total_rows, total_rows), 1)
    wanted = (spot % count) * parts + spot // count
    order = jnp.where(from_row == wanted, 1.0, 0.0).astype(BF16)
    rows_copy.wait()
    rows = rows_ref[...].astype(F32).reshape(total_rows, rows_ref.shape[2]).astype(BF16)
    rm_ref[...] = matmul(order, rows).astype(BF16)
    total = jnp.zeros((total_rows, we_ref.shape[1]), F32)
    for index in range(blocks):
        columns = slice(index * block, (index + 1) * block)
        if index + depth < blocks:
            copies[index + depth][0].start()
            copies[index + depth][1].start()
        copies[index][0].wait()
        lin = matmul(rm_ref[...], wh_ref[:, columns])
        value, slope = silu_parts(0.5 * lin)
        slope_ref[:, columns] = slope
        copies[index][1].wait()
        total = total + matmul(value.astype(BF16), we_ref[columns, :])
    summed = total[0:count]
    for part in range(1, parts):
        summed = summed + total[part * count : (part + 1) * count]
    out_ref[...] = summed


def encode(content, w_hidden, w_embed, block):
    count, parts, width = content.shape
    hidden = w_hidden.shape[1]
    model = w_embed.shape[1]
    return pl.pallas_call(
        functools.partial(encode_kernel, parts, block, 8),
        in_specs=[pl.BlockSpec(memory_space=pltpu.HBM)] * 3,
        out_specs=in_vmem(4),
        out_shape=[
            pltpu.VMEM((count * parts, hidden), F32),
            jax.ShapeDtypeStruct((count, model), F32),
            pltpu.VMEM(w_hidden.shape, BF16),
            pltpu.VMEM(w_embed.shape, BF16),
        ],
        scratch_shapes=[
            pltpu.VMEM(content.shape, BF16),
            pltpu.VMEM((count * parts, width), BF16),
            pltpu.SemaphoreType.DMA((2, hidden // block)),
            pltpu.SemaphoreType.DMA,
        ],
        compiler_params=params(16),
        name="encode",
    )(in_hbm(content), in_hbm(w_hidden), in_hbm(w_embed))


def warm_kernel(after_ref, cot_ref, wp_ref, key_hbm, value_hbm, og_ref, key_ref, value_ref, sems):
    copies = (
        pltpu.make_async_copy(key_hbm.at[0], key_ref, sems.at[0]),
        pltpu.make_async_copy(value_hbm.at[0], value_ref, sems.at[1]),
    )
    for copy in copies:
        copy.start()
    og_ref[...] = contract_last(cot_ref[...], wp_ref[...]).astype(BF16).astype(F32)
    for copy in copies:
        copy.wait()


def warm(after, cotangent, w_proj, keys, values):
    return pl.pallas_call(
        warm_kernel,
        in_specs=in_vmem(3) + [pl.BlockSpec(memory_space=pltpu.HBM)] * 2,
        out_specs=in_vmem(3),
        out_shape=[
            jax.ShapeDtypeStruct((cotangent.shape[0], w_proj.shape[0]), F32),
            pltpu.VMEM(keys.shape[1:], BF16),
            pltpu.VMEM(values.shape[1:], BF16),
        ],
        scratch_shapes=[pltpu.SemaphoreType.DMA((2,))],
        compiler_params=params(8),
        name="warm",
    )(after, cotangent, w_proj, in_hbm(keys), in_hbm(values))


def project_kernel(mine_ref, other_ref, wq_ref, wg_ref, og_ref, send_ref, ng_ref, qs_ref, gs_ref):
    embedded = (0.5 * (mine_ref[...] + other_ref[...])).astype(BF16)
    query, query_slope = silu_parts(0.5 * matmul(embedded, wq_ref[...]))
    gate, gate_slope = silu_parts(0.5 * matmul(embedded, wg_ref[...]))
    qs_ref[...] = 0.5 * query_slope
    gs_ref[...] = 0.5 * gate_slope
    ng_ref[...] = og_ref[...] * gate.astype(BF16).astype(F32)
    block = (query * (0.5 * DH ** (-0.5))).reshape(send_ref.shape[1:]).astype(BF16)
    for index in range(send_ref.shape[0]):
        send_ref[index] = block


def project(mine, other, w_query, w_gate, out_grad, copies, users):
    count = mine.shape[0]
    local = w_query.shape[1]
    rows = jax.ShapeDtypeStruct((count, local), F32)
    return pl.pallas_call(
        project_kernel,
        out_shape=[jax.ShapeDtypeStruct((copies, users, count // users, local), BF16)] + [rows] * 3,
        compiler_params=params(8),
        name="project",
    )(mine, other, w_query, w_gate, out_grad)


def forward_kernel(
    heads,
    block,
    query_ref,
    cutoff_ref,
    first_key_ref,
    first_value_ref,
    key_hbm,
    value_hbm,
    out_ref,
    slope_ref,
    key_ref,
    value_ref,
    limit_ref,
    sems,
):
    users, events = key_hbm.shape[0], key_hbm.shape[1]
    base = lax.axis_index("ctx") * events

    def fetch(user):
        return (
            pltpu.make_async_copy(key_hbm.at[user], key_ref.at[user - 1], sems.at[0, user - 1]),
            pltpu.make_async_copy(value_hbm.at[user], value_ref.at[user - 1], sems.at[1, user - 1]),
        )

    copies = {user: fetch(user) for user in range(1, users)}
    for user in range(1, users):
        for copy in copies[user]:
            copy.start()
    targets, local = query_ref.shape[0] * query_ref.shape[2], query_ref.shape[3]
    one = jnp.asarray(1.0, BF16)
    spots = lax.broadcasted_iota(jnp.int32, (targets, block), 1).astype(F32).astype(BF16)

    for user in range(users):
        queries = query_ref[:, pl.ds(user, 1)].astype(F32).reshape(targets, local).astype(BF16)
        limits = (cutoff_ref[pl.ds(user, 1), :] - base).astype(F32)
        limit_ref[...] = jnp.broadcast_to(limits, (block, targets)).T

        if user == 0:
            keys_here, values_here = first_key_ref, first_value_ref
        else:
            copies[user][0].wait()
            keys_here, values_here = key_ref.at[user - 1], value_ref.at[user - 1]
        totals = []
        for head in range(heads):
            lanes = slice(head * DH, (head + 1) * DH)
            weights = []
            for start in range(0, events, block):
                rows = slice(start, start + block)
                left = (limit_ref[...] - float(start)).astype(BF16)
                visible = spots < left
                half = contract_last(queries[:, lanes], keys_here[rows, lanes]).astype(BF16)
                tanh = jnp.where(visible, jnp.tanh(half), -one)
                lift = one + tanh
                weight = half * lift
                slope_ref[user, head, :, rows] = lift + weight * (one - tanh)
                weights.append(weight)
            if user > 0 and head == 0:
                copies[user][1].wait()
            totals.append(matmul(jnp.concatenate(weights, axis=-1), values_here[:, lanes]))
        total = jnp.concatenate(totals, axis=-1)
        out_ref[:, pl.ds(user, 1)] = total.reshape(-1, 1, query_ref.shape[2], local).astype(BF16)


def forward_attention(queries, cutoffs, first_keys, first_values, keys, values, heads):
    copies, users, rows, _ = queries.shape
    events = keys.shape[1]
    targets = copies * rows
    return pl.pallas_call(
        functools.partial(forward_kernel, heads, chunks_of(events)[0]),
        in_specs=in_vmem(4) + [pl.BlockSpec(memory_space=pltpu.HBM)] * 2,
        out_specs=in_vmem(4),
        out_shape=[
            jax.ShapeDtypeStruct(queries.shape, BF16),
            pltpu.VMEM((users, heads, targets, events), BF16),
            pltpu.VMEM((users - 1,) + keys.shape[1:], BF16),
            pltpu.VMEM((users - 1,) + values.shape[1:], BF16),
        ],
        scratch_shapes=[
            pltpu.VMEM((targets, chunks_of(events)[0]), F32),
            pltpu.SemaphoreType.DMA((2, users - 1)),
        ],
        compiler_params=params(16),
        name="attention_forward",
    )(
        queries,
        cutoffs,
        kept_in_vmem(first_keys),
        kept_in_vmem(first_values),
        in_hbm(keys),
        in_hbm(values),
    )


def norm_kernel(heads, parts_ref, ng_ref, og_ref, send_ref, gg_ref):
    total = parts_ref[0].astype(F32)
    for index in range(1, parts_ref.shape[0]):
        total = total + parts_ref[index].astype(F32)
    attended = total.reshape(ng_ref.shape)
    pieces = []
    for head in range(heads):
        lanes = slice(head * DH, (head + 1) * DH)
        rows = attended[:, lanes]
        rscale = lax.rsqrt(jnp.mean(rows * rows, axis=-1, keepdims=True) + 1e-06)
        normed = rows * rscale
        gg_ref[:, lanes] = og_ref[:, lanes] * normed
        normed_grad = ng_ref[:, lanes]
        mean = jnp.mean(normed_grad * normed, axis=-1, keepdims=True)
        pieces.append(rscale * (normed_grad - normed * mean))
    grad = jnp.concatenate(pieces, axis=-1)
    block = grad.reshape(send_ref.shape[1:]).astype(BF16)
    for index in range(send_ref.shape[0]):
        send_ref[index] = block


def norm_grads(partials, normed_grad, out_grad, heads):
    return pl.pallas_call(
        functools.partial(norm_kernel, heads),
        out_shape=[
            jax.ShapeDtypeStruct(partials.shape, BF16),
            jax.ShapeDtypeStruct(out_grad.shape, F32),
        ],
        compiler_params=params(8),
        name="norm_grads",
    )(partials, normed_grad, out_grad)


def backward_kernel(
    scale, heads, block, group, grad_ref, slope_ref, first_key_ref, first_value_ref, key_ref, value_ref, out_ref
):
    users, events = grad_ref.shape[1], key_ref.shape[1]
    targets, local = grad_ref.shape[0] * grad_ref.shape[2], grad_ref.shape[3]

    for user in range(users):
        if user == 0:
            keys_here, values_here = first_key_ref, first_value_ref
        else:
            keys_here, values_here = key_ref.at[user - 1], value_ref.at[user - 1]
        grads = grad_ref[:, pl.ds(user, 1)].astype(F32).reshape(targets, local).astype(BF16)
        totals = [jnp.zeros((targets, DH), F32) for _ in range(heads)]
        for first in range(0, events, block * group):
            span = slice(first, first + block * group)
            for head in range(heads):
                lanes = slice(head * DH, (head + 1) * DH)
                scored = []
                for start in range(first, first + block * group, block):
                    rows = slice(start, start + block)
                    weight_grad = contract_last(grads[:, lanes], values_here[rows, lanes])
                    scored.append(weight_grad.astype(BF16) * slope_ref[user, head, :, rows])
                totals[head] = totals[head] + matmul(
                    jnp.concatenate(scored, axis=-1), keys_here[span, lanes]
                )
        total = jnp.concatenate(totals, axis=-1) * (0.5 * scale)
        out_ref[:, pl.ds(user, 1)] = total.reshape(-1, 1, grad_ref.shape[2], local).astype(BF16)


def backward_attention(grads, slopes, history, heads):
    return pl.pallas_call(
        functools.partial(backward_kernel, DH ** (-0.5), heads, *chunks_of(slopes.shape[3])),
        in_specs=in_vmem(6),
        out_specs=in_vmem(1)[0],
        out_shape=jax.ShapeDtypeStruct(grads.shape, BF16),
        compiler_params=params(16),
        name="attention_backward",
    )(grads, kept_in_vmem(slopes), *map(kept_in_vmem, history))


def embed_kernel(parts_ref, gg_ref, qs_ref, gs_ref, wq_ref, wg_ref, out_ref):
    total = parts_ref[0].astype(F32)
    for index in range(1, parts_ref.shape[0]):
        total = total + parts_ref[index].astype(F32)
    query_back = (total.reshape(qs_ref.shape) * qs_ref[...]).astype(BF16)
    gate_back = (gg_ref[...] * gs_ref[...]).astype(BF16)
    out_ref[...] = contract_last(query_back, wq_ref[...]) + contract_last(gate_back, wg_ref[...])


def embed_grads(partials, gate_grad, query_slope, gate_slope, w_query, w_gate):
    return pl.pallas_call(
        embed_kernel,
        out_shape=jax.ShapeDtypeStruct((gate_grad.shape[0], w_query.shape[0]), F32),
        compiler_params=params(8),
        name="embed_grads",
    )(partials, gate_grad, query_slope, gate_slope, w_query, w_gate)


def content_first_kernel(parts, block, mine_ref, other_ref, we_ref, slope_ref, wh_ref, keep_ref, send_ref, back_ref):
    count = mine_ref.shape[0]
    half = parts // 2
    embed_grad = (0.5 * (mine_ref[...] + other_ref[...])).astype(BF16)
    hidden_grad = 0.5 * contract_last(embed_grad, we_ref[...])
    head = lax.axis_index("head")
    for index in range(parts):
        side = head if index < half else 1 - head
        source = pl.multiple_of((side * half + index % half) * count, count)
        back_ref[index * count : (index + 1) * count] = (
            hidden_grad * slope_ref[pl.ds(source, count), :]
        ).astype(BF16)
    content_columns(0, block, back_ref, wh_ref, keep_ref, send_ref)


def content_columns(first, block, back_ref, wh_ref, keep_ref, send_ref):
    kept, width = keep_ref.shape
    for start in range(0, width, block):
        columns = slice(start, start + block)
        part = contract_last(back_ref[...], wh_ref[first + start : first + start + block, :])
        keep_ref[:, columns] = part[:kept]
        send_ref[:, columns] = part[kept:].astype(BF16)


def content_second_kernel(block, back_ref, wh_ref, keep_ref, send_ref):
    content_columns(wh_ref.shape[0] // 2, block, back_ref, wh_ref, keep_ref, send_ref)


def content_first(mine, other, w_embed, slopes, w_hidden, parts, block):
    count, hidden = slopes.shape
    shape = (count // 2, w_hidden.shape[0] // 2)
    return pl.pallas_call(
        functools.partial(content_first_kernel, parts, block),
        in_specs=in_vmem(5),
        out_specs=in_vmem(3),
        out_shape=[
            jax.ShapeDtypeStruct(shape, F32),
            jax.ShapeDtypeStruct(shape, BF16),
            pltpu.VMEM((count, hidden), BF16),
        ],
        compiler_params=params(16),
        name="content_first",
    )(mine, other, kept_in_vmem(w_embed), kept_in_vmem(slopes), kept_in_vmem(w_hidden))


def content_second(back, w_hidden, block):
    shape = (back.shape[0] // 2, w_hidden.shape[0] // 2)
    return pl.pallas_call(
        functools.partial(content_second_kernel, block),
        in_specs=in_vmem(2),
        out_specs=in_vmem(2),
        out_shape=[
            jax.ShapeDtypeStruct(shape, F32),
            jax.ShapeDtypeStruct(shape, BF16),
        ],
        compiler_params=params(16),
        name="content_second",
    )(kept_in_vmem(back), kept_in_vmem(w_hidden))


def placed_rows(keep_ref, got_ref, count, half):
    rows = count * half
    spot = lax.broadcasted_iota(jnp.int32, (rows, rows), 0)
    from_row = lax.broadcasted_iota(jnp.int32, (rows, rows), 1)
    order = jnp.where(from_row == (spot % half) * count + spot // half, 1.0, 0.0).astype(BF16)
    total = (keep_ref[...] + got_ref[...].astype(F32)).astype(BF16)
    return matmul(order, total).reshape(count, half, -1).astype(BF16)


def place_kernel(keep_ref, got_ref, out_ref):
    out_ref[...] = placed_rows(keep_ref, got_ref, *out_ref.shape[:2])


def place(keep, got, count, half):
    return pl.pallas_call(
        place_kernel,
        in_specs=in_vmem(2),
        out_specs=in_vmem(1)[0],
        out_shape=pltpu.VMEM((count, half, keep.shape[1]), BF16),
        compiler_params=params(8),
        name="place",
    )(keep, got)


def finish_kernel(first_ref, keep_ref, got_ref, out_hbm, last_ref, sems):
    width = first_ref.shape[2]
    early = pltpu.make_async_copy(first_ref, out_hbm.at[:, :, pl.ds(0, width)], sems.at[0])
    early.start()
    last_ref[...] = placed_rows(keep_ref, got_ref, *first_ref.shape[:2])
    late = pltpu.make_async_copy(last_ref, out_hbm.at[:, :, pl.ds(width, width)], sems.at[1])
    late.start()
    early.wait()
    late.wait()


def finish(first, keep, got):
    count, half, width = first.shape
    return pl.pallas_call(
        finish_kernel,
        in_specs=in_vmem(3),
        out_specs=pl.BlockSpec(memory_space=pltpu.HBM),
        out_shape=jax.ShapeDtypeStruct((count, half, 2 * width), BF16),
        scratch_shapes=[pltpu.VMEM(first.shape, BF16), pltpu.SemaphoreType.DMA((2,))],
        compiler_params=params(8),
        name="finish",
    )(kept_in_vmem(first), keep, got)


def body(
    head_count,
    content_rows,
    w_hidden,
    w_embed,
    w_query,
    w_gate,
    w_proj,
    history_keys,
    history_values,
    cutoffs,
    out_cotangent,
):
    users, shard_rows, parts, width = content_rows.shape
    local = w_query.shape[1]
    heads = local // DH
    count = users * shard_rows
    copies = cutoffs.shape[1] // shard_rows
    swap = [(index, (index + 1) % head_count) for index in range(head_count)]

    def to_owner(blocks):
        return lax.all_to_all(blocks, "ctx", 0, 0, tiled=True)

    hidden_slope, mine, w_hidden, w_embed = encode(
        content_rows.reshape(count, parts, width), w_hidden, w_embed, 256
    )
    other = lax.ppermute(mine, "head", swap)
    cotangent = out_cotangent.reshape(count, -1)
    out_grad, first_keys, first_values = warm(mine, cotangent, w_proj, history_keys, history_values)
    sends, normed_grad, query_slope, gate_slope = project(
        mine, other, w_query, w_gate, out_grad, copies, users
    )
    partial, slopes, rest_keys, rest_values = forward_attention(
        to_owner(sends), cutoffs, first_keys, first_values, history_keys, history_values, heads
    )
    sends, gate_grad = norm_grads(to_owner(partial), normed_grad, out_grad, heads)
    history = (first_keys, first_values, rest_keys, rest_values)
    partial = backward_attention(to_owner(sends), slopes, history, heads)
    mine = embed_grads(to_owner(partial), gate_grad, query_slope, gate_slope, w_query, w_gate)
    other = lax.ppermute(mine, "head", swap)
    keep1, send1, back = content_first(mine, other, w_embed, hidden_slope, w_hidden, parts, 256)
    got1 = lax.ppermute(send1, "head", swap)
    keep2, send2 = content_second(back, w_hidden, 256)
    half = parts // head_count
    got2 = lax.ppermute(send2, "head", swap)
    first = place(keep1, got1, count, half)
    total = finish(first, keep2, got2)
    return total.reshape(users, shard_rows, half, width)


def solution(mesh):
    in_specs = (
        P(None, "ctx", None, None),
        P(None, "head"),
        P("head", None),
        P(None, "head"),
        P(None, "head"),
        P("head", None),
        P(None, "ctx", "head"),
        P(None, "ctx", "head"),
        P(),
        P(None, "ctx", None),
    )
    out_specs = P(None, "ctx", "head", None)
    return jax.shard_map(
        functools.partial(body, mesh.shape["head"]),
        mesh=mesh,
        in_specs=in_specs,
        out_specs=out_specs,
        check_vma=False,
    )
```

```python
import functools

import jax
import jax.numpy as jnp
from jax import lax
from jax.experimental import pallas as pl
from jax.experimental.pallas import tpu as pltpu
from jax.sharding import PartitionSpec as P


DH = 128
F32 = jnp.float32
BF16 = jnp.bfloat16
GROUP = 9


def matmul(left, right):
    return jnp.dot(left, right, preferred_element_type=F32)


def contract_last(left, right):
    return lax.dot_general(left, right, (((1,), (1,)), ((), ())), preferred_element_type=F32)


def silu_parts(half):
    tanh = jnp.tanh(half)
    lift = 1.0 + tanh
    value = half * lift
    return value, lift + value * (1.0 - tanh)


def params(mebibytes):
    return pltpu.CompilerParams(vmem_limit_bytes=mebibytes << 20)


def in_vmem(count):
    return [pl.BlockSpec(memory_space=pltpu.VMEM)] * count


def in_hbm(array):
    return pltpu.with_memory_space_constraint(array, pltpu.HBM)


def kept_in_vmem(array):
    return pltpu.with_memory_space_constraint(array, pltpu.VMEM)


def chunks_of(length):
    block = 256
    while length % block:
        block //= 2
    group = GROUP
    while (length // block) % group:
        group -= 1
    return block, group


def encode_kernel(
    parts, block, depth, rows_hbm, wh_hbm, we_hbm, slope_ref, out_ref, wh_ref, we_ref, rows_ref, rm_ref, sems, row_sem
):
    total_rows, hidden = slope_ref.shape
    blocks = hidden // block
    count = total_rows // parts
    copies = []
    for index in range(blocks):
        columns = pl.ds(index * block, block)
        copies.append(
            (
                pltpu.make_async_copy(wh_hbm.at[:, columns], wh_ref.at[:, columns], sems.at[0, index]),
                pltpu.make_async_copy(we_hbm.at[columns, :], we_ref.at[columns, :], sems.at[1, index]),
            )
        )
    rows_copy = pltpu.make_async_copy(rows_hbm, rows_ref, row_sem)
    rows_copy.start()
    copies[0][0].start()
    spot = lax.broadcasted_iota(jnp.int32, (total_rows, total_rows), 0)
    from_row = lax.broadcasted_iota(jnp.int32, (total_rows, total_rows), 1)
    wanted = (spot % count) * parts + spot // count
    order = jnp.where(from_row == wanted, 1.0, 0.0).astype(BF16)
    rows_copy.wait()
    copies[0][1].start()
    for pair in copies[1:depth]:
        pair[0].start()
        pair[1].start()
    rows = rows_ref[...].astype(F32).reshape(total_rows, rows_ref.shape[2]).astype(BF16)
    rm_ref[...] = matmul(order, rows).astype(BF16)
    total = jnp.zeros((total_rows, we_ref.shape[1]), F32)
    for index in range(blocks):
        columns = slice(index * block, (index + 1) * block)
        if index + depth < blocks:
            copies[index + depth][0].start()
            copies[index + depth][1].start()
        copies[index][0].wait()
        lin = matmul(rm_ref[...], wh_ref[:, columns])
        value, slope = silu_parts(0.5 * lin)
        slope_ref[:, columns] = slope
        copies[index][1].wait()
        total = total + matmul(value.astype(BF16), we_ref[columns, :])
    summed = total[0:count]
    for part in range(1, parts):
        summed = summed + total[part * count : (part + 1) * count]
    out_ref[...] = summed


def encode(content, w_hidden, w_embed, block):
    count, parts, width = content.shape
    hidden = w_hidden.shape[1]
    model = w_embed.shape[1]
    return pl.pallas_call(
        functools.partial(encode_kernel, parts, block, 4),
        in_specs=[pl.BlockSpec(memory_space=pltpu.HBM)] * 3,
        out_specs=in_vmem(4),
        out_shape=[
            pltpu.VMEM((count * parts, hidden), F32),
            jax.ShapeDtypeStruct((count, model), F32),
            pltpu.VMEM(w_hidden.shape, BF16),
            pltpu.VMEM(w_embed.shape, BF16),
        ],
        scratch_shapes=[
            pltpu.VMEM(content.shape, BF16),
            pltpu.VMEM((count * parts, width), BF16),
            pltpu.SemaphoreType.DMA((2, hidden // block)),
            pltpu.SemaphoreType.DMA,
        ],
        compiler_params=params(16),
        name="encode",
    )(in_hbm(content), in_hbm(w_hidden), in_hbm(w_embed))


def warm_kernel(after_ref, cot_ref, wp_ref, key_hbm, value_hbm, og_ref, key_ref, value_ref, sems):
    copies = (
        pltpu.make_async_copy(key_hbm.at[0], key_ref, sems.at[0]),
        pltpu.make_async_copy(value_hbm.at[0], value_ref, sems.at[1]),
    )
    for copy in copies:
        copy.start()
    og_ref[...] = contract_last(cot_ref[...], wp_ref[...]).astype(BF16).astype(F32)
    for copy in copies:
        copy.wait()


def warm(after, cotangent, w_proj, keys, values):
    return pl.pallas_call(
        warm_kernel,
        in_specs=in_vmem(3) + [pl.BlockSpec(memory_space=pltpu.HBM)] * 2,
        out_specs=in_vmem(3),
        out_shape=[
            jax.ShapeDtypeStruct((cotangent.shape[0], w_proj.shape[0]), F32),
            pltpu.VMEM(keys.shape[1:], BF16),
            pltpu.VMEM(values.shape[1:], BF16),
        ],
        scratch_shapes=[pltpu.SemaphoreType.DMA((2,))],
        compiler_params=params(8),
        name="warm",
    )(after, cotangent, w_proj, in_hbm(keys), in_hbm(values))


def project_kernel(mine_ref, other_ref, wq_ref, wg_ref, og_ref, send_ref, ng_ref, qs_ref, gs_ref):
    embedded = (0.5 * (mine_ref[...] + other_ref[...])).astype(BF16)
    query, query_slope = silu_parts(0.5 * matmul(embedded, wq_ref[...]))
    gate, gate_slope = silu_parts(0.5 * matmul(embedded, wg_ref[...]))
    qs_ref[...] = 0.5 * query_slope
    gs_ref[...] = 0.5 * gate_slope
    ng_ref[...] = og_ref[...] * gate.astype(BF16).astype(F32)
    block = (query * (0.5 * DH ** (-0.5))).reshape(send_ref.shape[1:]).astype(BF16)
    for index in range(send_ref.shape[0]):
        send_ref[index] = block


def project(mine, other, w_query, w_gate, out_grad, copies, users):
    count = mine.shape[0]
    local = w_query.shape[1]
    rows = jax.ShapeDtypeStruct((count, local), F32)
    return pl.pallas_call(
        project_kernel,
        out_shape=[jax.ShapeDtypeStruct((copies, users, count // users, local), BF16)] + [rows] * 3,
        compiler_params=params(8),
        name="project",
    )(mine, other, w_query, w_gate, out_grad)


def forward_kernel(
    heads,
    block,
    group,
    query_ref,
    cutoff_ref,
    first_key_ref,
    first_value_ref,
    key_hbm,
    value_hbm,
    out_ref,
    slope_ref,
    key_ref,
    value_ref,
    limit_ref,
    sems,
):
    users, events = key_hbm.shape[0], key_hbm.shape[1]
    base = lax.axis_index("ctx") * events

    def fetch(user):
        return (
            pltpu.make_async_copy(key_hbm.at[user], key_ref.at[user - 1], sems.at[0, user - 1]),
            pltpu.make_async_copy(value_hbm.at[user], value_ref.at[user - 1], sems.at[1, user - 1]),
        )

    for user in range(1, min(3, users)):
        for copy in fetch(user):
            copy.start()
    targets, local = query_ref.shape[0] * query_ref.shape[2], query_ref.shape[3]
    one = jnp.asarray(1.0, BF16)
    spots = lax.broadcasted_iota(jnp.int32, (targets, block), 1).astype(F32).astype(BF16)

    for user in range(users):
        queries = query_ref[:, pl.ds(user, 1)].astype(F32).reshape(targets, local).astype(BF16)
        limits = (cutoff_ref[pl.ds(user, 1), :] - base).astype(F32)
        limit_ref[...] = jnp.broadcast_to(limits, (block, targets)).T

        if user == 0:
            keys_here, values_here = first_key_ref, first_value_ref
        else:
            if user + 2 < users:
                for copy in fetch(user + 2):
                    copy.start()
            for copy in fetch(user):
                copy.wait()
            keys_here, values_here = key_ref.at[user - 1], value_ref.at[user - 1]
        totals = [jnp.zeros((targets, DH), F32) for _ in range(heads)]
        for first in range(0, events, block * group):
            span = slice(first, first + block * group)
            for head in range(heads):
                lanes = slice(head * DH, (head + 1) * DH)
                weights = []
                for start in range(first, first + block * group, block):
                    rows = slice(start, start + block)
                    left = (limit_ref[...] - float(start)).astype(BF16)
                    visible = spots < left
                    half = contract_last(queries[:, lanes], keys_here[rows, lanes]).astype(BF16)
                    tanh = jnp.where(visible, jnp.tanh(half), -one)
                    lift = one + tanh
                    weight = half * lift
                    slope_ref[user, head, :, rows] = lift + weight * (one - tanh)
                    weights.append(weight)
                totals[head] = totals[head] + matmul(
                    jnp.concatenate(weights, axis=-1), values_here[span, lanes]
                )
        total = jnp.concatenate(totals, axis=-1)
        out_ref[:, pl.ds(user, 1)] = total.reshape(-1, 1, query_ref.shape[2], local).astype(BF16)


def forward_attention(queries, cutoffs, first_keys, first_values, keys, values, heads):
    copies, users, rows, _ = queries.shape
    events = keys.shape[1]
    targets = copies * rows
    return pl.pallas_call(
        functools.partial(forward_kernel, heads, *chunks_of(events)),
        in_specs=in_vmem(4) + [pl.BlockSpec(memory_space=pltpu.HBM)] * 2,
        out_specs=in_vmem(4),
        out_shape=[
            jax.ShapeDtypeStruct(queries.shape, BF16),
            pltpu.VMEM((users, heads, targets, events), BF16),
            pltpu.VMEM((users - 1,) + keys.shape[1:], BF16),
            pltpu.VMEM((users - 1,) + values.shape[1:], BF16),
        ],
        scratch_shapes=[
            pltpu.VMEM((targets, chunks_of(events)[0]), F32),
            pltpu.SemaphoreType.DMA((2, users - 1)),
        ],
        compiler_params=params(16),
        name="attention_forward",
    )(
        queries,
        cutoffs,
        kept_in_vmem(first_keys),
        kept_in_vmem(first_values),
        in_hbm(keys),
        in_hbm(values),
    )


def norm_kernel(heads, parts_ref, ng_ref, og_ref, send_ref, gg_ref):
    total = parts_ref[0].astype(F32)
    for index in range(1, parts_ref.shape[0]):
        total = total + parts_ref[index].astype(F32)
    attended = total.reshape(ng_ref.shape)
    pieces = []
    for head in range(heads):
        lanes = slice(head * DH, (head + 1) * DH)
        rows = attended[:, lanes]
        rscale = lax.rsqrt(jnp.mean(rows * rows, axis=-1, keepdims=True) + 1e-06)
        normed = rows * rscale
        gg_ref[:, lanes] = og_ref[:, lanes] * normed
        normed_grad = ng_ref[:, lanes]
        mean = jnp.mean(normed_grad * normed, axis=-1, keepdims=True)
        pieces.append(rscale * (normed_grad - normed * mean))
    grad = jnp.concatenate(pieces, axis=-1)
    block = grad.reshape(send_ref.shape[1:]).astype(BF16)
    for index in range(send_ref.shape[0]):
        send_ref[index] = block


def norm_grads(partials, normed_grad, out_grad, heads):
    return pl.pallas_call(
        functools.partial(norm_kernel, heads),
        out_shape=[
            jax.ShapeDtypeStruct(partials.shape, BF16),
            jax.ShapeDtypeStruct(out_grad.shape, F32),
        ],
        compiler_params=params(8),
        name="norm_grads",
    )(partials, normed_grad, out_grad)


def backward_kernel(
    scale, heads, block, group, grad_ref, slope_ref, first_key_ref, first_value_ref, key_ref, value_ref, out_ref
):
    users, events = grad_ref.shape[1], key_ref.shape[1]
    targets, local = grad_ref.shape[0] * grad_ref.shape[2], grad_ref.shape[3]

    for user in range(users):
        if user == 0:
            keys_here, values_here = first_key_ref, first_value_ref
        else:
            keys_here, values_here = key_ref.at[user - 1], value_ref.at[user - 1]
        grads = grad_ref[:, pl.ds(user, 1)].astype(F32).reshape(targets, local).astype(BF16)
        totals = [jnp.zeros((targets, DH), F32) for _ in range(heads)]
        for first in range(0, events, block * group):
            span = slice(first, first + block * group)
            for head in range(heads):
                lanes = slice(head * DH, (head + 1) * DH)
                scored = []
                for start in range(first, first + block * group, block):
                    rows = slice(start, start + block)
                    weight_grad = contract_last(grads[:, lanes], values_here[rows, lanes])
                    scored.append(weight_grad.astype(BF16) * slope_ref[user, head, :, rows])
                totals[head] = totals[head] + matmul(
                    jnp.concatenate(scored, axis=-1), keys_here[span, lanes]
                )
        total = jnp.concatenate(totals, axis=-1) * (0.5 * scale)
        out_ref[:, pl.ds(user, 1)] = total.reshape(-1, 1, grad_ref.shape[2], local).astype(BF16)


def backward_attention(grads, slopes, history, heads):
    return pl.pallas_call(
        functools.partial(backward_kernel, DH ** (-0.5), heads, *chunks_of(slopes.shape[3])),
        in_specs=in_vmem(6),
        out_specs=in_vmem(1)[0],
        out_shape=jax.ShapeDtypeStruct(grads.shape, BF16),
        compiler_params=params(16),
        name="attention_backward",
    )(grads, kept_in_vmem(slopes), *map(kept_in_vmem, history))


def embed_kernel(parts_ref, gg_ref, qs_ref, gs_ref, wq_ref, wg_ref, out_ref):
    total = parts_ref[0].astype(F32)
    for index in range(1, parts_ref.shape[0]):
        total = total + parts_ref[index].astype(F32)
    query_back = (total.reshape(qs_ref.shape) * qs_ref[...]).astype(BF16)
    gate_back = (gg_ref[...] * gs_ref[...]).astype(BF16)
    out_ref[...] = contract_last(query_back, wq_ref[...]) + contract_last(gate_back, wg_ref[...])


def embed_grads(partials, gate_grad, query_slope, gate_slope, w_query, w_gate):
    return pl.pallas_call(
        embed_kernel,
        out_shape=jax.ShapeDtypeStruct((gate_grad.shape[0], w_query.shape[0]), F32),
        compiler_params=params(8),
        name="embed_grads",
    )(partials, gate_grad, query_slope, gate_slope, w_query, w_gate)


def content_first_kernel(parts, block, mine_ref, other_ref, we_ref, slope_ref, wh_ref, keep_ref, send_ref, back_ref):
    count = mine_ref.shape[0]
    half = parts // 2
    embed_grad = (0.5 * (mine_ref[...] + other_ref[...])).astype(BF16)
    hidden_grad = 0.5 * contract_last(embed_grad, we_ref[...])
    head = lax.axis_index("head")
    for index in range(parts):
        side = head if index < half else 1 - head
        source = pl.multiple_of((side * half + index % half) * count, count)
        back_ref[index * count : (index + 1) * count] = (
            hidden_grad * slope_ref[pl.ds(source, count), :]
        ).astype(BF16)
    content_columns(0, block, back_ref, wh_ref, keep_ref, send_ref)


def content_columns(first, block, back_ref, wh_ref, keep_ref, send_ref):
    kept, width = keep_ref.shape
    for start in range(0, width, block):
        columns = slice(start, start + block)
        part = contract_last(back_ref[...], wh_ref[first + start : first + start + block, :])
        keep_ref[:, columns] = part[:kept]
        send_ref[:, columns] = part[kept:].astype(BF16)


def content_second_kernel(block, back_ref, wh_ref, keep_ref, send_ref):
    content_columns(wh_ref.shape[0] // 2, block, back_ref, wh_ref, keep_ref, send_ref)


def content_first(mine, other, w_embed, slopes, w_hidden, parts, block):
    count, hidden = slopes.shape
    shape = (count // 2, w_hidden.shape[0] // 2)
    return pl.pallas_call(
        functools.partial(content_first_kernel, parts, block),
        in_specs=in_vmem(5),
        out_specs=in_vmem(3),
        out_shape=[
            jax.ShapeDtypeStruct(shape, F32),
            jax.ShapeDtypeStruct(shape, BF16),
            pltpu.VMEM((count, hidden), BF16),
        ],
        compiler_params=params(16),
        name="content_first",
    )(mine, other, kept_in_vmem(w_embed), kept_in_vmem(slopes), kept_in_vmem(w_hidden))


def content_second(back, w_hidden, block):
    shape = (back.shape[0] // 2, w_hidden.shape[0] // 2)
    return pl.pallas_call(
        functools.partial(content_second_kernel, block),
        in_specs=in_vmem(2),
        out_specs=in_vmem(2),
        out_shape=[
            jax.ShapeDtypeStruct(shape, F32),
            jax.ShapeDtypeStruct(shape, BF16),
        ],
        compiler_params=params(16),
        name="content_second",
    )(kept_in_vmem(back), kept_in_vmem(w_hidden))


def placed_rows(keep_ref, got_ref, count, half):
    rows = count * half
    spot = lax.broadcasted_iota(jnp.int32, (rows, rows), 0)
    from_row = lax.broadcasted_iota(jnp.int32, (rows, rows), 1)
    order = jnp.where(from_row == (spot % half) * count + spot // half, 1.0, 0.0).astype(BF16)
    total = (keep_ref[...] + got_ref[...].astype(F32)).astype(BF16)
    return matmul(order, total).reshape(count, half, -1).astype(BF16)


def place_kernel(keep_ref, got_ref, out_ref):
    out_ref[...] = placed_rows(keep_ref, got_ref, *out_ref.shape[:2])


def place(keep, got, count, half):
    return pl.pallas_call(
        place_kernel,
        in_specs=in_vmem(2),
        out_specs=in_vmem(1)[0],
        out_shape=pltpu.VMEM((count, half, keep.shape[1]), BF16),
        compiler_params=params(8),
        name="place",
    )(keep, got)


def finish_kernel(first_ref, keep_ref, got_ref, out_hbm, last_ref, sems):
    width = first_ref.shape[2]
    early = pltpu.make_async_copy(first_ref, out_hbm.at[:, :, pl.ds(0, width)], sems.at[0])
    early.start()
    last_ref[...] = placed_rows(keep_ref, got_ref, *first_ref.shape[:2])
    late = pltpu.make_async_copy(last_ref, out_hbm.at[:, :, pl.ds(width, width)], sems.at[1])
    late.start()
    early.wait()
    late.wait()


def finish(first, keep, got):
    count, half, width = first.shape
    return pl.pallas_call(
        finish_kernel,
        in_specs=in_vmem(3),
        out_specs=pl.BlockSpec(memory_space=pltpu.HBM),
        out_shape=jax.ShapeDtypeStruct((count, half, 2 * width), BF16),
        scratch_shapes=[pltpu.VMEM(first.shape, BF16), pltpu.SemaphoreType.DMA((2,))],
        compiler_params=params(8),
        name="finish",
    )(kept_in_vmem(first), keep, got)


def body(
    head_count,
    content_rows,
    w_hidden,
    w_embed,
    w_query,
    w_gate,
    w_proj,
    history_keys,
    history_values,
    cutoffs,
    out_cotangent,
):
    users, shard_rows, parts, width = content_rows.shape
    local = w_query.shape[1]
    heads = local // DH
    count = users * shard_rows
    copies = cutoffs.shape[1] // shard_rows
    swap = [(index, (index + 1) % head_count) for index in range(head_count)]

    def to_owner(blocks):
        return lax.all_to_all(blocks, "ctx", 0, 0, tiled=True)

    hidden_slope, mine, w_hidden, w_embed = encode(
        content_rows.reshape(count, parts, width), w_hidden, w_embed, 512
    )
    other = lax.ppermute(mine, "head", swap)
    cotangent = out_cotangent.reshape(count, -1)
    out_grad, first_keys, first_values = warm(mine, cotangent, w_proj, history_keys, history_values)
    sends, normed_grad, query_slope, gate_slope = project(
        mine, other, w_query, w_gate, out_grad, copies, users
    )
    partial, slopes, rest_keys, rest_values = forward_attention(
        to_owner(sends), cutoffs, first_keys, first_values, history_keys, history_values, heads
    )
    sends, gate_grad = norm_grads(to_owner(partial), normed_grad, out_grad, heads)
    history = (first_keys, first_values, rest_keys, rest_values)
    partial = backward_attention(to_owner(sends), slopes, history, heads)
    mine = embed_grads(to_owner(partial), gate_grad, query_slope, gate_slope, w_query, w_gate)
    other = lax.ppermute(mine, "head", swap)
    keep1, send1, back = content_first(mine, other, w_embed, hidden_slope, w_hidden, parts, 256)
    got1 = lax.ppermute(send1, "head", swap)
    keep2, send2 = content_second(back, w_hidden, 256)
    half = parts // head_count
    got2 = lax.ppermute(send2, "head", swap)
    first = place(keep1, got1, count, half)
    total = finish(first, keep2, got2)
    return total.reshape(users, shard_rows, half, width)


def solution(mesh):
    in_specs = (
        P(None, "ctx", None, None),
        P(None, "head"),
        P("head", None),
        P(None, "head"),
        P(None, "head"),
        P("head", None),
        P(None, "ctx", "head"),
        P(None, "ctx", "head"),
        P(),
        P(None, "ctx", None),
    )
    out_specs = P(None, "ctx", "head", None)
    return jax.shard_map(
        functools.partial(body, mesh.shape["head"]),
        mesh=mesh,
        in_specs=in_specs,
        out_specs=out_specs,
        check_vma=False,
    )
```

```python
import functools

import jax
import jax.numpy as jnp
from jax import lax
from jax.experimental import pallas as pl
from jax.experimental.pallas import tpu as pltpu
from jax.sharding import PartitionSpec as P


DH = 128
F32 = jnp.float32
BF16 = jnp.bfloat16
GROUP = 9


def matmul(left, right):
    return jnp.dot(left, right, preferred_element_type=F32)


def contract_last(left, right):
    return lax.dot_general(left, right, (((1,), (1,)), ((), ())), preferred_element_type=F32)


def silu_parts(half):
    tanh = jnp.tanh(half)
    lift = 1.0 + tanh
    value = half * lift
    return value, lift + value * (1.0 - tanh)


def params(mebibytes):
    return pltpu.CompilerParams(vmem_limit_bytes=mebibytes << 20)


def in_vmem(count):
    return [pl.BlockSpec(memory_space=pltpu.VMEM)] * count


def in_hbm(array):
    return pltpu.with_memory_space_constraint(array, pltpu.HBM)


def kept_in_vmem(array):
    return pltpu.with_memory_space_constraint(array, pltpu.VMEM)


def chunks_of(length):
    block = 256
    while length % block:
        block //= 2
    group = GROUP
    while (length // block) % group:
        group -= 1
    return block, group


def encode_kernel(
    parts, block, depth, rows_hbm, wh_hbm, we_hbm, slope_ref, out_ref, wh_ref, we_ref, rows_ref, rm_ref, sems, row_sem
):
    total_rows, hidden = slope_ref.shape
    blocks = hidden // block
    count = total_rows // parts
    copies = []
    for index in range(blocks):
        columns = pl.ds(index * block, block)
        copies.append(
            (
                pltpu.make_async_copy(wh_hbm.at[:, columns], wh_ref.at[:, columns], sems.at[0, index]),
                pltpu.make_async_copy(we_hbm.at[columns, :], we_ref.at[columns, :], sems.at[1, index]),
            )
        )
    rows_copy = pltpu.make_async_copy(rows_hbm, rows_ref, row_sem)
    rows_copy.start()
    copies[0][0].start()
    spot = lax.broadcasted_iota(jnp.int32, (total_rows, total_rows), 0)
    from_row = lax.broadcasted_iota(jnp.int32, (total_rows, total_rows), 1)
    wanted = (spot % count) * parts + spot // count
    order = jnp.where(from_row == wanted, 1.0, 0.0).astype(BF16)
    rows_copy.wait()
    copies[0][1].start()
    for pair in copies[1:depth]:
        pair[0].start()
        pair[1].start()
    rows = rows_ref[...].astype(F32).reshape(total_rows, rows_ref.shape[2]).astype(BF16)
    rm_ref[...] = matmul(order, rows).astype(BF16)
    total = jnp.zeros((total_rows, we_ref.shape[1]), F32)
    for index in range(blocks):
        columns = slice(index * block, (index + 1) * block)
        if index + depth < blocks:
            copies[index + depth][0].start()
            copies[index + depth][1].start()
        copies[index][0].wait()
        lin = matmul(rm_ref[...], wh_ref[:, columns])
        value, slope = silu_parts(0.5 * lin)
        slope_ref[:, columns] = slope
        copies[index][1].wait()
        total = total + matmul(value.astype(BF16), we_ref[columns, :])
    summed = total[0:count]
    for part in range(1, parts):
        summed = summed + total[part * count : (part + 1) * count]
    out_ref[...] = summed


def encode(content, w_hidden, w_embed, block):
    count, parts, width = content.shape
    hidden = w_hidden.shape[1]
    model = w_embed.shape[1]
    return pl.pallas_call(
        functools.partial(encode_kernel, parts, block, 4),
        in_specs=[pl.BlockSpec(memory_space=pltpu.HBM)] * 3,
        out_specs=in_vmem(4),
        out_shape=[
            pltpu.VMEM((count * parts, hidden), F32),
            jax.ShapeDtypeStruct((count, model), F32),
            pltpu.VMEM(w_hidden.shape, BF16),
            pltpu.VMEM(w_embed.shape, BF16),
        ],
        scratch_shapes=[
            pltpu.VMEM(content.shape, BF16),
            pltpu.VMEM((count * parts, width), BF16),
            pltpu.SemaphoreType.DMA((2, hidden // block)),
            pltpu.SemaphoreType.DMA,
        ],
        compiler_params=params(16),
        name="encode",
    )(in_hbm(content), in_hbm(w_hidden), in_hbm(w_embed))


def warm_kernel(after_ref, cot_ref, wp_ref, key_hbm, value_hbm, og_ref, key_ref, value_ref, sems):
    copies = (
        pltpu.make_async_copy(key_hbm.at[0], key_ref, sems.at[0]),
        pltpu.make_async_copy(value_hbm.at[0], value_ref, sems.at[1]),
    )
    for copy in copies:
        copy.start()
    og_ref[...] = contract_last(cot_ref[...], wp_ref[...]).astype(BF16).astype(F32)
    for copy in copies:
        copy.wait()


def warm(after, cotangent, w_proj, keys, values):
    return pl.pallas_call(
        warm_kernel,
        in_specs=in_vmem(3) + [pl.BlockSpec(memory_space=pltpu.HBM)] * 2,
        out_specs=in_vmem(3),
        out_shape=[
            jax.ShapeDtypeStruct((cotangent.shape[0], w_proj.shape[0]), F32),
            pltpu.VMEM(keys.shape[1:], BF16),
            pltpu.VMEM(values.shape[1:], BF16),
        ],
        scratch_shapes=[pltpu.SemaphoreType.DMA((2,))],
        compiler_params=params(8),
        name="warm",
    )(after, cotangent, w_proj, in_hbm(keys), in_hbm(values))


def project_kernel(mine_ref, other_ref, wq_ref, wg_ref, og_ref, send_ref, ng_ref, qs_ref, gs_ref):
    embedded = (0.5 * (mine_ref[...] + other_ref[...])).astype(BF16)
    query, query_slope = silu_parts(0.5 * matmul(embedded, wq_ref[...]))
    gate, gate_slope = silu_parts(0.5 * matmul(embedded, wg_ref[...]))
    qs_ref[...] = 0.5 * query_slope
    gs_ref[...] = 0.5 * gate_slope
    ng_ref[...] = og_ref[...] * gate.astype(BF16).astype(F32)
    block = (query * (0.5 * DH ** (-0.5))).reshape(send_ref.shape[1:]).astype(BF16)
    for index in range(send_ref.shape[0]):
        send_ref[index] = block


def project(mine, other, w_query, w_gate, out_grad, copies, users):
    count = mine.shape[0]
    local = w_query.shape[1]
    rows = jax.ShapeDtypeStruct((count, local), F32)
    return pl.pallas_call(
        project_kernel,
        out_shape=[jax.ShapeDtypeStruct((copies, users, count // users, local), BF16)] + [rows] * 3,
        compiler_params=params(8),
        name="project",
    )(mine, other, w_query, w_gate, out_grad)


def forward_kernel(
    heads,
    block,
    group,
    query_ref,
    cutoff_ref,
    first_key_ref,
    first_value_ref,
    key_hbm,
    value_hbm,
    out_ref,
    slope_ref,
    key_ref,
    value_ref,
    limit_ref,
    sems,
):
    users, events = key_hbm.shape[0], key_hbm.shape[1]
    base = lax.axis_index("ctx") * events

    def fetch(user):
        return (
            pltpu.make_async_copy(key_hbm.at[user], key_ref.at[user - 1], sems.at[0, user - 1]),
            pltpu.make_async_copy(value_hbm.at[user], value_ref.at[user - 1], sems.at[1, user - 1]),
        )

    for user in range(1, min(3, users)):
        for copy in fetch(user):
            copy.start()
    targets, local = query_ref.shape[0] * query_ref.shape[2], query_ref.shape[3]
    one = jnp.asarray(1.0, BF16)
    spots = lax.broadcasted_iota(jnp.int32, (targets, block), 1).astype(F32).astype(BF16)

    for user in range(users):
        queries = query_ref[:, pl.ds(user, 1)].astype(F32).reshape(targets, local).astype(BF16)
        limits = (cutoff_ref[pl.ds(user, 1), :] - base).astype(F32)
        limit_ref[...] = jnp.broadcast_to(limits, (block, targets)).T

        if user == 0:
            keys_here, values_here = first_key_ref, first_value_ref
        else:
            if user + 2 < users:
                for copy in fetch(user + 2):
                    copy.start()
            for copy in fetch(user):
                copy.wait()
            keys_here, values_here = key_ref.at[user - 1], value_ref.at[user - 1]
        totals = [jnp.zeros((targets, DH), F32) for _ in range(heads)]
        for first in range(0, events, block * group):
            span = slice(first, first + block * group)
            for head in range(heads):
                lanes = slice(head * DH, (head + 1) * DH)
                weights = []
                for start in range(first, first + block * group, block):
                    rows = slice(start, start + block)
                    left = (limit_ref[...] - float(start)).astype(BF16)
                    visible = spots < left
                    half = contract_last(queries[:, lanes], keys_here[rows, lanes]).astype(BF16)
                    tanh = jnp.where(visible, jnp.tanh(half), -one)
                    lift = one + tanh
                    weight = half * lift
                    slope_ref[user, head, :, rows] = lift + weight * (one - tanh)
                    weights.append(weight)
                totals[head] = totals[head] + matmul(
                    jnp.concatenate(weights, axis=-1), values_here[span, lanes]
                )
        total = jnp.concatenate(totals, axis=-1)
        out_ref[:, pl.ds(user, 1)] = total.reshape(-1, 1, query_ref.shape[2], local).astype(BF16)


def forward_attention(queries, cutoffs, first_keys, first_values, keys, values, heads):
    copies, users, rows, _ = queries.shape
    events = keys.shape[1]
    targets = copies * rows
    return pl.pallas_call(
        functools.partial(forward_kernel, heads, *chunks_of(events)),
        in_specs=in_vmem(4) + [pl.BlockSpec(memory_space=pltpu.HBM)] * 2,
        out_specs=in_vmem(4),
        out_shape=[
            jax.ShapeDtypeStruct(queries.shape, BF16),
            pltpu.VMEM((users, heads, targets, events), BF16),
            pltpu.VMEM((users - 1,) + keys.shape[1:], BF16),
            pltpu.VMEM((users - 1,) + values.shape[1:], BF16),
        ],
        scratch_shapes=[
            pltpu.VMEM((targets, chunks_of(events)[0]), F32),
            pltpu.SemaphoreType.DMA((2, users - 1)),
        ],
        compiler_params=params(16),
        name="attention_forward",
    )(
        queries,
        cutoffs,
        kept_in_vmem(first_keys),
        kept_in_vmem(first_values),
        in_hbm(keys),
        in_hbm(values),
    )


def norm_kernel(heads, parts_ref, ng_ref, og_ref, send_ref, gg_ref):
    total = parts_ref[0].astype(F32)
    for index in range(1, parts_ref.shape[0]):
        total = total + parts_ref[index].astype(F32)
    attended = total.reshape(ng_ref.shape)
    pieces = []
    for head in range(heads):
        lanes = slice(head * DH, (head + 1) * DH)
        rows = attended[:, lanes]
        rscale = lax.rsqrt(jnp.mean(rows * rows, axis=-1, keepdims=True) + 1e-06)
        normed = rows * rscale
        gg_ref[:, lanes] = og_ref[:, lanes] * normed
        normed_grad = ng_ref[:, lanes]
        mean = jnp.mean(normed_grad * normed, axis=-1, keepdims=True)
        pieces.append(rscale * (normed_grad - normed * mean))
    grad = jnp.concatenate(pieces, axis=-1)
    block = grad.reshape(send_ref.shape[1:]).astype(BF16)
    for index in range(send_ref.shape[0]):
        send_ref[index] = block


def norm_grads(partials, normed_grad, out_grad, heads):
    return pl.pallas_call(
        functools.partial(norm_kernel, heads),
        out_shape=[
            jax.ShapeDtypeStruct(partials.shape, BF16),
            jax.ShapeDtypeStruct(out_grad.shape, F32),
        ],
        compiler_params=params(8),
        name="norm_grads",
    )(partials, normed_grad, out_grad)


def backward_kernel(
    scale, heads, block, group, grad_ref, slope_ref, first_key_ref, first_value_ref, key_ref, value_ref, out_ref
):
    users, events = grad_ref.shape[1], key_ref.shape[1]
    targets, local = grad_ref.shape[0] * grad_ref.shape[2], grad_ref.shape[3]

    for user in range(users):
        if user == 0:
            keys_here, values_here = first_key_ref, first_value_ref
        else:
            keys_here, values_here = key_ref.at[user - 1], value_ref.at[user - 1]
        grads = grad_ref[:, pl.ds(user, 1)].astype(F32).reshape(targets, local).astype(BF16)
        totals = [jnp.zeros((targets, DH), F32) for _ in range(heads)]
        for first in range(0, events, block * group):
            span = slice(first, first + block * group)
            for head in range(heads):
                lanes = slice(head * DH, (head + 1) * DH)
                scored = []
                for start in range(first, first + block * group, block):
                    rows = slice(start, start + block)
                    weight_grad = contract_last(grads[:, lanes], values_here[rows, lanes])
                    scored.append(weight_grad.astype(BF16) * slope_ref[user, head, :, rows])
                totals[head] = totals[head] + matmul(
                    jnp.concatenate(scored, axis=-1), keys_here[span, lanes]
                )
        total = jnp.concatenate(totals, axis=-1) * (0.5 * scale)
        out_ref[:, pl.ds(user, 1)] = total.reshape(-1, 1, grad_ref.shape[2], local).astype(BF16)


def backward_attention(grads, slopes, history, heads):
    return pl.pallas_call(
        functools.partial(backward_kernel, DH ** (-0.5), heads, *chunks_of(slopes.shape[3])),
        in_specs=in_vmem(6),
        out_specs=in_vmem(1)[0],
        out_shape=jax.ShapeDtypeStruct(grads.shape, BF16),
        compiler_params=params(16),
        name="attention_backward",
    )(grads, kept_in_vmem(slopes), *map(kept_in_vmem, history))


def embed_kernel(parts_ref, gg_ref, qs_ref, gs_ref, wq_ref, wg_ref, out_ref, send_ref):
    total = parts_ref[0].astype(F32)
    for index in range(1, parts_ref.shape[0]):
        total = total + parts_ref[index].astype(F32)
    query_back = (total.reshape(qs_ref.shape) * qs_ref[...]).astype(BF16)
    gate_back = (gg_ref[...] * gs_ref[...]).astype(BF16)
    part = contract_last(query_back, wq_ref[...]) + contract_last(gate_back, wg_ref[...])
    out_ref[...] = part
    send_ref[...] = part.astype(BF16)


def embed_grads(partials, gate_grad, query_slope, gate_slope, w_query, w_gate):
    return pl.pallas_call(
        embed_kernel,
        out_shape=[jax.ShapeDtypeStruct((gate_grad.shape[0], w_query.shape[0]), kind) for kind in (F32, BF16)],
        compiler_params=params(8),
        name="embed_grads",
    )(partials, gate_grad, query_slope, gate_slope, w_query, w_gate)


def content_first_kernel(parts, block, mine_ref, other_ref, we_ref, slope_ref, wh_ref, keep_ref, send_ref, back_ref):
    count = mine_ref.shape[0]
    half = parts // 2
    embed_grad = (0.5 * (mine_ref[...] + other_ref[...].astype(F32))).astype(BF16)
    hidden_grad = 0.5 * contract_last(embed_grad, we_ref[...])
    head = lax.axis_index("head")
    for index in range(parts):
        side = head if index < half else 1 - head
        source = pl.multiple_of((side * half + index % half) * count, count)
        back_ref[index * count : (index + 1) * count] = (
            hidden_grad * slope_ref[pl.ds(source, count), :]
        ).astype(BF16)
    content_columns(0, block, back_ref, wh_ref, keep_ref, send_ref)


def content_columns(first, block, back_ref, wh_ref, keep_ref, send_ref):
    kept, width = keep_ref.shape
    for start in range(0, width, block):
        columns = slice(start, start + block)
        part = contract_last(back_ref[...], wh_ref[first + start : first + start + block, :])
        keep_ref[:, columns] = part[:kept]
        send_ref[:, columns] = part[kept:].astype(BF16)


def content_second_kernel(block, back_ref, wh_ref, keep_ref, send_ref):
    content_columns(wh_ref.shape[0] - keep_ref.shape[1], block, back_ref, wh_ref, keep_ref, send_ref)


def content_first(mine, other, w_embed, slopes, w_hidden, parts, block, early):
    count, hidden = slopes.shape
    shape = (count // 2, early)
    return pl.pallas_call(
        functools.partial(content_first_kernel, parts, block),
        in_specs=in_vmem(5),
        out_specs=in_vmem(3),
        out_shape=[
            jax.ShapeDtypeStruct(shape, F32),
            jax.ShapeDtypeStruct(shape, BF16),
            pltpu.VMEM((count, hidden), BF16),
        ],
        compiler_params=params(16),
        name="content_first",
    )(mine, other, kept_in_vmem(w_embed), kept_in_vmem(slopes), kept_in_vmem(w_hidden))


def content_second(back, w_hidden, block, early):
    shape = (back.shape[0] // 2, w_hidden.shape[0] - early)
    return pl.pallas_call(
        functools.partial(content_second_kernel, block),
        in_specs=in_vmem(2),
        out_specs=in_vmem(2),
        out_shape=[
            jax.ShapeDtypeStruct(shape, F32),
            jax.ShapeDtypeStruct(shape, BF16),
        ],
        compiler_params=params(16),
        name="content_second",
    )(kept_in_vmem(back), kept_in_vmem(w_hidden))


def placed_rows(keep_ref, got_ref, count, half):
    rows = count * half
    spot = lax.broadcasted_iota(jnp.int32, (rows, rows), 0)
    from_row = lax.broadcasted_iota(jnp.int32, (rows, rows), 1)
    order = jnp.where(from_row == (spot % half) * count + spot // half, 1.0, 0.0).astype(BF16)
    total = (keep_ref[...] + got_ref[...].astype(F32)).astype(BF16)
    return matmul(order, total).reshape(count, half, -1).astype(BF16)


def place_kernel(keep_ref, got_ref, out_ref):
    out_ref[...] = placed_rows(keep_ref, got_ref, *out_ref.shape[:2])


def place(keep, got, count, half):
    return pl.pallas_call(
        place_kernel,
        in_specs=in_vmem(2),
        out_specs=in_vmem(1)[0],
        out_shape=pltpu.VMEM((count, half, keep.shape[1]), BF16),
        compiler_params=params(8),
        name="place",
    )(keep, got)


def finish_kernel(first_ref, keep_ref, got_ref, out_hbm, last_ref, sems):
    width, rest = first_ref.shape[2], last_ref.shape[2]
    early = pltpu.make_async_copy(first_ref, out_hbm.at[:, :, pl.ds(0, width)], sems.at[0])
    early.start()
    last_ref[...] = placed_rows(keep_ref, got_ref, *first_ref.shape[:2])
    late = pltpu.make_async_copy(last_ref, out_hbm.at[:, :, pl.ds(width, rest)], sems.at[1])
    late.start()
    early.wait()
    late.wait()


def finish(first, keep, got):
    count, half, width = first.shape
    rest = keep.shape[1]
    return pl.pallas_call(
        finish_kernel,
        in_specs=in_vmem(3),
        out_specs=pl.BlockSpec(memory_space=pltpu.HBM),
        out_shape=jax.ShapeDtypeStruct((count, half, width + rest), BF16),
        scratch_shapes=[pltpu.VMEM((count, half, rest), BF16), pltpu.SemaphoreType.DMA((2,))],
        compiler_params=params(8),
        name="finish",
    )(kept_in_vmem(first), keep, got)


def body(
    head_count,
    content_rows,
    w_hidden,
    w_embed,
    w_query,
    w_gate,
    w_proj,
    history_keys,
    history_values,
    cutoffs,
    out_cotangent,
):
    users, shard_rows, parts, width = content_rows.shape
    local = w_query.shape[1]
    heads = local // DH
    count = users * shard_rows
    copies = cutoffs.shape[1] // shard_rows
    swap = [(index, (index + 1) % head_count) for index in range(head_count)]

    def to_owner(blocks):
        return lax.all_to_all(blocks, "ctx", 0, 0, tiled=True)

    hidden_slope, mine, w_hidden, w_embed = encode(
        content_rows.reshape(count, parts, width), w_hidden, w_embed, 512
    )
    other = lax.ppermute(mine, "head", swap)
    cotangent = out_cotangent.reshape(count, -1)
    out_grad, first_keys, first_values = warm(mine, cotangent, w_proj, history_keys, history_values)
    sends, normed_grad, query_slope, gate_slope = project(
        mine, other, w_query, w_gate, out_grad, copies, users
    )
    partial, slopes, rest_keys, rest_values = forward_attention(
        to_owner(sends), cutoffs, first_keys, first_values, history_keys, history_values, heads
    )
    sends, gate_grad = norm_grads(to_owner(partial), normed_grad, out_grad, heads)
    history = (first_keys, first_values, rest_keys, rest_values)
    partial = backward_attention(to_owner(sends), slopes, history, heads)
    mine, send = embed_grads(to_owner(partial), gate_grad, query_slope, gate_slope, w_query, w_gate)
    other = lax.ppermute(send, "head", swap)
    early = width * 5 // 8
    keep1, send1, back = content_first(mine, other, w_embed, hidden_slope, w_hidden, parts, 256, early)
    got1 = lax.ppermute(send1, "head", swap)
    keep2, send2 = content_second(back, w_hidden, 256, early)
    half = parts // head_count
    got2 = lax.ppermute(send2, "head", swap)
    first = place(keep1, got1, count, half)
    total = finish(first, keep2, got2)
    return total.reshape(users, shard_rows, half, width)


def solution(mesh):
    in_specs = (
        P(None, "ctx", None, None),
        P(None, "head"),
        P("head", None),
        P(None, "head"),
        P(None, "head"),
        P("head", None),
        P(None, "ctx", "head"),
        P(None, "ctx", "head"),
        P(),
        P(None, "ctx", None),
    )
    out_specs = P(None, "ctx", "head", None)
    return jax.shard_map(
        functools.partial(body, mesh.shape["head"]),
        mesh=mesh,
        in_specs=in_specs,
        out_specs=out_specs,
        check_vma=False,
    )
```
